128 devices in a mesh: frame: 8 (over y_lo, z), patch: 16 (over y_hi, x, core).
Axes of the slice: x: 4, y: 4 (y_hi: 2, y_lo: 2; y = y_hi * 2 + y_lo), z: 4, core: 2. Of those that a mesh axis runs over, the one named last changes fastest.
Arguments:
- query_rows: bfloat16 [32, 1024, 1408], P('frame', 'patch'), may hold values from -6 to 6, as said below
- key_rows: bfloat16 [32, 1024, 1408], P('frame', 'patch'), may hold values from -6 to 6, as said below
- value_rows: bfloat16 [32, 1024, 1408], P('frame', 'patch'), may hold values from -6 to 6
- grad_out: bfloat16 [32, 1024, 1408], P('frame', 'patch'), may hold values from -6 to 6
- out_weight: bfloat16 [1408, 1408], replicated, may hold values from -0.15625 to 0.15625
Outputs:
- grad_query: bfloat16 [32, 1024, 1408], P('frame', 'patch')
- grad_key: bfloat16 [32, 1024, 1408], P('frame', 'patch')
- grad_value: bfloat16 [32, 1024, 1408], P('frame', 'patch')
- grad_weight: float32 [1408, 1408], P(('frame', 'patch'))
The draws below stay inside these ranges and needn't reach their ends.
Inputs may be any that keep to these rules, and one draw needn't show every extreme that they name: `query_rows`: entries of order one. `key_rows`: entries of order one.
All inputs are finite; a program needn't handle non-finite values.
Results may differ from the reference program's by a relative error of at most 0.017.
Values may be sent and summed in bfloat16 or wider, within the bound.
No kernel may reach another device: no remote copies, remote signals or barrier semaphores. Data moves between devices by JAX's collectives and lax.ppermute only.
A program may use at most 128 MiB of HBM per device.

```python
import jax
import jax.numpy as jnp
from jax import lax

D = 1408
HEADS = 16
HEAD_DIM = 88
PATCHES = 1024
FRAMES = 32


def draw_pair(key):
    full_shape = (FRAMES, PATCHES, D)
    base_key = jax.random.fold_in(key, 41)
    key_query, key_keys = jax.random.split(base_key, 2)
    queries = jnp.clip(jax.random.normal(key_query, full_shape, jnp.float32), -4.0, 4.0)
    keyset = jnp.clip(jax.random.normal(key_keys, full_shape, jnp.float32), -4.0, 4.0)
    return (queries, keyset)


def draw_query_rows(key, part):
    return draw_pair(key)[0].astype(jnp.bfloat16)


def draw_key_rows(key, part):
    return draw_pair(key)[1].astype(jnp.bfloat16)


def with_spikes(values, key, source, target, parts, factor):
    def block_of(dim):
        return (jnp.arange(values.shape[dim]) // (values.shape[dim] // parts)).reshape((-1,) + (1,) * (values.ndim - 1 - dim))

    first = jax.random.permutation(key, parts)[block_of(target)]
    far = (block_of(target) + parts // 2) % parts
    return jnp.where((block_of(source) == first) | (block_of(source) == far), factor * values, values)


def shard_levels(key, shape, cuts, low, largest):
    def one(dim, parts):
        steps = jax.random.uniform(jax.random.fold_in(jax.random.fold_in(key, 6), dim), (parts,), jnp.float32, low / len(cuts), largest / len(cuts))
        return jnp.repeat(jnp.exp(steps), shape[dim] // parts).reshape((-1,) + (1,) * (len(shape) - dim - 1))

    loudness = one(*cuts[0])
    for cut in cuts[1:]:
        loudness = loudness * one(*cut)
    return loudness


def scatter_about(own_key, extent, width, limit, cuts=(), kind=jnp.bfloat16):
    drawn = width * jax.random.normal(own_key, extent, jnp.float32)
    if cuts:
        drawn = drawn * shard_levels(own_key, extent, cuts, -0.22, 0.18)
    return jnp.clip(drawn, -limit, limit).astype(kind)


def gaussian_with(own_key, dims, scale, bound, cuts, heavy, held_as=jnp.bfloat16):
    values = scale * jax.random.normal(own_key, dims, jnp.float32)
    if cuts:
        values = values * shard_levels(own_key, dims, cuts, -0.22, 0.18)
    return jnp.clip(with_spikes(values, jax.random.fold_in(own_key, 3), *heavy), -bound, bound).astype(held_as)


def setup_inputs(seed: int = 0) -> dict:
    key_list = jax.random.split(jax.random.key(seed), 6)
    query_rows = draw_query_rows(jax.random.fold_in(key_list[5], 71), 0)
    key_rows = draw_key_rows(jax.random.fold_in(key_list[5], 71), 0)
    value_rows = scatter_about(key_list[2], (FRAMES, PATCHES, D), 1.0, 6.0, ((0, 8), (1, 16)))
    grad_out = gaussian_with(key_list[3], (FRAMES, PATCHES, D), 1.0, 6.0, ((0, 8), (1, 16)), (1, 2, 16, 2.0))
    out_weight = scatter_about(key_list[4], (D, D), D ** -0.5, 0.15625)
    return {"query_rows": query_rows, "key_rows": key_rows, "value_rows": value_rows, "grad_out": grad_out, "out_weight": out_weight}


def frame_backward(pieces):
    query_part, key_part, value_part, upstream = pieces
    softmax_scale = HEAD_DIM ** -0.5
    query_heads = query_part.reshape(PATCHES, HEADS, HEAD_DIM).astype(jnp.float32)
    key_heads = key_part.reshape(PATCHES, HEADS, HEAD_DIM).astype(jnp.float32)
    value_heads = value_part.reshape(PATCHES, HEADS, HEAD_DIM).astype(jnp.float32)
    upstream_heads = upstream.reshape(PATCHES, HEADS, HEAD_DIM).astype(jnp.float32)
    scores = jnp.einsum("qhd,khd->hqk", query_heads, key_heads) * softmax_scale
    row_max = jnp.max(scores, axis=-1, keepdims=True)
    raised = jnp.exp(scores - row_max)
    weights = raised / jnp.sum(raised, axis=-1, keepdims=True)
    weights_low = weights.astype(jnp.bfloat16).astype(jnp.float32)
    attended = jnp.einsum("hqk,khd->qhd", weights_low, value_heads).astype(jnp.bfloat16)
    grad_weights = jnp.einsum("qhd,khd->hqk", upstream_heads, value_heads)
    row_dot = jnp.sum(upstream_heads * attended.astype(jnp.float32), axis=-1)
    grad_scores = (weights * (grad_weights - jnp.transpose(row_dot)[:, :, None])).astype(jnp.bfloat16).astype(jnp.float32)
    grad_query = (jnp.einsum("hqk,khd->qhd", grad_scores, key_heads) * softmax_scale).astype(jnp.bfloat16)
    grad_key = (jnp.einsum("hqk,qhd->khd", grad_scores, query_heads) * softmax_scale).astype(jnp.bfloat16)
    grad_value = jnp.einsum("hqk,qhd->khd", weights_low, upstream_heads).astype(jnp.bfloat16)
    return (grad_query.reshape(PATCHES, D), grad_key.reshape(PATCHES, D),
            grad_value.reshape(PATCHES, D), attended.reshape(PATCHES, D))


def reference(query_rows, key_rows, value_rows, grad_out, out_weight):
    flat_grad = grad_out.reshape(FRAMES * PATCHES, D)
    grad_attn = jnp.dot(flat_grad, out_weight, preferred_element_type=jnp.float32).astype(jnp.bfloat16)
    grad_attn = grad_attn.reshape(FRAMES, PATCHES, D)
    grad_query, grad_key, grad_value, attended = lax.map(frame_backward, (query_rows, key_rows, value_rows, grad_attn))
    grad_weight = jnp.dot(flat_grad.T, attended.reshape(FRAMES * PATCHES, D), preferred_element_type=jnp.float32)
    return grad_query, grad_key, grad_value, grad_weight
```

```python
import functools

import jax
import jax.numpy as jnp
from jax import lax
from jax.experimental import pallas as pl
from jax.experimental.pallas import tpu as pltpu
from jax.sharding import Mesh, PartitionSpec as P

HEAD_DIM = 88
HEADS = 16
HALF = 64
BLOCK = 256
SOFTMAX_SCALE = HEAD_DIM ** (-0.5)
EXP2_SCALE = SOFTMAX_SCALE * 1.4426950408889634
F32, BF16 = jnp.float32, jnp.bfloat16


def head_of(slot):
    return 8 * (slot % 2) + slot // 2


def low_lanes(shape):
    return lax.broadcasted_iota(jnp.int32, shape, 1) < HALF


def turned(tile):
    return pltpu.roll(tile, HALF, 1)


def frame_pair(ref, n):
    first, second = [], []
    for s in range(8):
        a, b = ref[s, n].astype(F32), ref[s + 8, n].astype(F32)
        low = low_lanes(a.shape)
        first.append(jnp.where(low, a, turned(b)).astype(BF16))
        second.append(jnp.where(low, turned(a), b).astype(BF16))
    return jnp.concatenate(first, 1), jnp.concatenate(second, 1)


def put_back(ref, n, first, second):
    for s in range(8):
        a, b = first[:, 128 * s : 128 * (s + 1)], second[:, 128 * s : 128 * (s + 1)]
        low = low_lanes(a.shape)
        ref[s, n] = jnp.where(low, a, turned(b)).astype(BF16)
        ref[s + 8, n] = jnp.where(low, turned(a), b).astype(BF16)


def pack_kernel(q_ref, k_ref, v_ref, g_ref, w_hbm, out_ref, w_ref, sem):
    fetch = pltpu.make_async_copy(w_hbm, w_ref, sem)
    fetch.start()

    def place(n, rows):
        turned_rows = rows.T
        for slot in range(HEADS):
            at = HEAD_DIM * head_of(slot)
            out_ref[slot, n] = turned_rows[at : at + HEAD_DIM].astype(BF16)

    features = q_ref.shape[-1]
    for n, ref in enumerate((q_ref, k_ref, v_ref)):
        place(n, ref[...].reshape(-1, features))
    fetch.wait()
    place(
        3,
        jnp.dot(g_ref[...].reshape(-1, features), w_ref[...], preferred_element_type=F32).astype(BF16),
    )


def pack(query, key, value, upstream, weight):
    tokens = query.shape[0] * query.shape[1]
    return pl.pallas_call(
        pack_kernel,
        in_specs=[pl.BlockSpec(memory_space=pltpu.VMEM)] * 4 + [pl.BlockSpec(memory_space=pl.ANY)],
        out_specs=pl.BlockSpec(memory_space=pltpu.VMEM),
        out_shape=jax.ShapeDtypeStruct((HEADS, 4, HEAD_DIM, tokens), BF16),
        scratch_shapes=[pltpu.VMEM(weight.shape, BF16), pltpu.SemaphoreType.DMA],
        cost_estimate=pl.CostEstimate(flops=2 * tokens * weight.size, bytes_accessed=10_000_000, transcendentals=0),
        name="pack_by_head",
    )(query, key, value, upstream, weight)


def forward_kernel(x_ref, att_ref, e_ref, inv_ref, o_ref):
    qs, ks, vs = (frame_pair(x_ref, n) for n in range(3))
    for f in range(2):
        q_t, k, v_t = qs[f], ks[f].T, vs[f]
        for b in range(1024 // BLOCK):
            cols = slice(b * BLOCK, (b + 1) * BLOCK)
            scores = jnp.dot(k, q_t[:, cols], preferred_element_type=F32)
            row_max = jnp.max(scores, axis=0, keepdims=True)
            raised = jnp.exp2(scores * EXP2_SCALE - row_max * EXP2_SCALE)
            inverse = 1.0 / jnp.sum(raised, axis=0, keepdims=True)
            raised = raised.astype(BF16)
            e_ref[f, :, cols] = raised
            o_ref[f, :, cols] = jnp.dot(v_t, raised, preferred_element_type=F32) * inverse
            inv_ref[f, :, cols] = jnp.broadcast_to(inverse, (8, BLOCK))
    put_back(att_ref, 0, o_ref[0], o_ref[1])


PAIR = pl.BlockSpec((HEADS, 4, HEAD_DIM, 128), lambda i: (0, 0, 0, i))
ONE = pl.BlockSpec((HEADS, 1, HEAD_DIM, 128), lambda i: (0, 0, 0, i))
RAISED = pl.BlockSpec((2, 1024, 1024), lambda i: (i, 0, 0))
INVERSE = pl.BlockSpec((2, 8, 1024), lambda i: (i, 0, 0))


def forward(x):
    return pl.pallas_call(
        forward_kernel,
        grid=(2,),
        in_specs=[PAIR],
        out_specs=[ONE, RAISED, INVERSE],
        out_shape=[
            jax.ShapeDtypeStruct((HEADS, 1, HEAD_DIM, 256), BF16),
            jax.ShapeDtypeStruct((4, 1024, 1024), BF16),
            jax.ShapeDtypeStruct((4, 8, 1024), F32),
        ],
        scratch_shapes=[pltpu.VMEM((2, HEAD_DIM, 1024), F32)],
        cost_estimate=pl.CostEstimate(flops=4 * 4 * 1024 * 1024 * 256, bytes_accessed=12_000_000, transcendentals=1 << 22),
        name="spatial_forward",
    )(x)


def backward_kernel(x_ref, att_ref, e_ref, inv_ref, out_ref, dq_ref, dk_ref, dv_ref):
    qs, ks, vs, gs = (frame_pair(x_ref, n) for n in range(4))
    os = frame_pair(att_ref, 0)
    for f in range(2):
        q_t, k_t, v = qs[f], ks[f], vs[f].T
        scaled = gs[f].astype(F32) * inv_ref[f, 0:1, :]
        row_dot = jnp.sum(scaled * os[f].astype(F32), axis=0, keepdims=True)
        g_t = scaled.astype(BF16)
        for b in range(1024 // BLOCK):
            cols = slice(b * BLOCK, (b + 1) * BLOCK)
            raised = e_ref[f, :, cols]
            grad_probs = jnp.dot(v, g_t[:, cols], preferred_element_type=F32)
            grad_scores = (raised.astype(F32) * (grad_probs - row_dot[:, cols])).astype(BF16)
            dq_ref[f, :, cols] = jnp.dot(k_t, grad_scores, preferred_element_type=F32) * SOFTMAX_SCALE
            dk = lax.dot_general(q_t[:, cols], grad_scores, (((1,), (1,)), ((), ())), preferred_element_type=F32)
            dv = lax.dot_general(g_t[:, cols], raised, (((1,), (1,)), ((), ())), preferred_element_type=F32)
            if b == 0:
                dk_ref[f], dv_ref[f] = dk, dv
            else:
                dk_ref[f] += dk
                dv_ref[f] += dv
    put_back(out_ref, 0, dq_ref[0], dq_ref[1])
    put_back(out_ref, 1, dk_ref[0] * SOFTMAX_SCALE, dk_ref[1] * SOFTMAX_SCALE)
    put_back(out_ref, 2, dv_ref[0], dv_ref[1])


def backward(x, attended, raised, inverse):
    return pl.pallas_call(
        backward_kernel,
        grid=(2,),
        in_specs=[PAIR, ONE, RAISED, INVERSE],
        out_specs=pl.BlockSpec((HEADS, 3, HEAD_DIM, 128), lambda i: (0, 0, 0, i)),
        out_shape=jax.ShapeDtypeStruct((HEADS, 3, HEAD_DIM, 256), BF16),
        scratch_shapes=[pltpu.VMEM((2, HEAD_DIM, 1024), F32)] * 3,
        cost_estimate=pl.CostEstimate(flops=8 * 4 * 1024 * 1024 * 256, bytes_accessed=14_000_000, transcendentals=0),
        name="spatial_backward",
    )(x, attended, raised, inverse)


def weight_kernel(place_ref, mine_ref, other_ref, att_ref, o0, o1, o2, o3, g_ref, a_ref):
    core, z = place_ref[0], place_ref[1]
    features = mine_ref.shape[-1]
    g_ref[:, :256] = mine_ref[...].reshape(-1, features).T
    g_ref[:, 256:] = other_ref[...].reshape(-1, features).T
    for i in range(8):
        rows = slice(HEAD_DIM * i, HEAD_DIM * (i + 1))
        a_ref[rows, :256] = att_ref[i, core]
        a_ref[rows, 256:] = att_ref[i, 1 - core]
    att = a_ref[...]
    for r, out in enumerate((o0, o1, o2, o3)):
        for half in range(2):
            block = half * 4 + lax.rem(z + r, 4)
            rows = pl.ds(pl.multiple_of(block * 176, 16), 176)
            out[half] = lax.dot_general(
                g_ref[rows, :], att, (((1,), (1,)), ((), ())), preferred_element_type=F32
            ).astype(out.dtype)


def weight_terms(place, mine, other, att):
    features = mine.shape[-1]
    return pl.pallas_call(
        weight_kernel,
        in_specs=[pl.BlockSpec(memory_space=pltpu.SMEM)] + [pl.BlockSpec(memory_space=pltpu.VMEM)] * 3,
        out_specs=[pl.BlockSpec(memory_space=pltpu.VMEM)] * 4,
        out_shape=[jax.ShapeDtypeStruct((2, 176, 704), BF16)] * 4,
        scratch_shapes=[pltpu.VMEM((features, 512), BF16), pltpu.VMEM((704, 512), BF16)],
        cost_estimate=pl.CostEstimate(flops=2 * 512 * 1408 * 704, bytes_accessed=5_000_000, transcendentals=0),
        name="weight_terms",
    )(place, mine, other, att)


def rows_kernel(a, b, c, d, out):
    total = a[...].astype(F32) + b[...].astype(F32) + c[...].astype(F32) + d[...].astype(F32)
    total = total.reshape(352, 704)
    for p in range(32):
        out[p] = total[11 * p : 11 * (p + 1)].astype(BF16)


def row_sums(parts):
    return pl.pallas_call(
        rows_kernel,
        in_specs=[pl.BlockSpec(memory_space=pltpu.VMEM)] * 4,
        out_specs=pl.BlockSpec(memory_space=pltpu.VMEM),
        out_shape=jax.ShapeDtypeStruct((32, 11, 704), BF16),
        cost_estimate=pl.CostEstimate(flops=1_000_000, bytes_accessed=3_000_000, transcendentals=0),
        name="row_sums",
    )(*parts)


def unpack_kernel(x_ref, q_ref, k_ref, v_ref, t_ref):
    for n, ref in enumerate((q_ref, k_ref, v_ref)):
        for slot in range(HEADS):
            at = HEAD_DIM * head_of(slot)
            t_ref[at : at + HEAD_DIM] = x_ref[slot, n]
        ref[...] = t_ref[...].T.reshape(ref.shape)


def unpack(x, shape):
    return pl.pallas_call(
        unpack_kernel,
        in_specs=[pl.BlockSpec(memory_space=pltpu.VMEM)],
        out_specs=[pl.BlockSpec(memory_space=pltpu.VMEM)] * 3,
        out_shape=[jax.ShapeDtypeStruct(shape, BF16)] * 3,
        scratch_shapes=[pltpu.VMEM((shape[-1], shape[0] * shape[1]), BF16)],
        cost_estimate=pl.CostEstimate(flops=0, bytes_accessed=5_000_000, transcendentals=0),
        name="unpack_by_token",
    )(x)


FRAME, PATCH = ("y_lo", "z"), ("y_hi", "x", "core")
PLANE = ("y_lo", "y_hi", "x", "core")


def exchange(array, axes):
    return lax.all_to_all(array, axes, split_axis=0, concat_axis=0, tiled=True)


def along_z(array, step):
    return lax.ppermute(array, "z", [(i, (i + step) % 4) for i in range(4)])


def shards(query_rows, key_rows, value_rows, grad_out, out_weight):
    place = jnp.stack([lax.axis_index("core"), lax.axis_index("z")]).astype(jnp.int32)
    other_grad = lax.ppermute(grad_out, "core", [(0, 1), (1, 0)])
    x = exchange(pack(query_rows, key_rows, value_rows, grad_out, out_weight), PATCH)
    attended, raised, inverse = forward(x)
    att = exchange(attended.reshape(8, 2, HEAD_DIM, 256), ("y_hi", "x"))
    grads = backward(x, attended, raised, inverse)
    own, *sent = weight_terms(place, grad_out, other_grad, att)
    parts = [own] + [along_z(part, step + 1) for step, part in enumerate(sent)]
    outs = unpack(exchange(grads, PATCH), query_rows.shape)
    rows = exchange(row_sums(parts), PLANE)
    total = rows.reshape(16, 2, 11, 704).astype(F32).sum(0)
    grad_weight = jnp.concatenate([total[0], total[1]], axis=1)
    return (*outs, grad_weight)


def solution(mesh):
    chips = Mesh(mesh.devices.reshape(2, 4, 2, 4, 2), FRAME + PATCH)
    rows = P(FRAME, PATCH, None)
    return jax.shard_map(
        shards,
        mesh=chips,
        in_specs=(rows, rows, rows, rows, P()),
        out_specs=(rows, rows, rows, P(FRAME + PATCH, None)),
        check_vma=False,
    )
```

```python
import jax
import jax.numpy as jnp
from jax import lax
from jax.experimental import pallas as pl
from jax.experimental.pallas import tpu as pltpu
from jax.sharding import Mesh, PartitionSpec as P


HEAD_DIM = 88
HEADS = 16
HALF = 64
BLOCK = 256
SOFTMAX_SCALE = HEAD_DIM ** (-0.5)
EXP2_SCALE = SOFTMAX_SCALE * 1.4426950408889634
F32, BF16 = jnp.float32, jnp.bfloat16


def head_of(slot):
    return 8 * (slot % 2) + slot // 2


def low_lanes(shape):
    return lax.broadcasted_iota(jnp.int32, shape, 1) < HALF


def turned(tile):
    return pltpu.roll(tile, HALF, 1)


def frame_pair(ref, n):
    first, second = [], []
    for s in range(8):
        a, b = ref[s, n].astype(F32), ref[s + 8, n].astype(F32)
        low = low_lanes(a.shape)
        first.append(jnp.where(low, a, turned(b)).astype(BF16))
        second.append(jnp.where(low, turned(a), b).astype(BF16))
    return jnp.concatenate(first, 1), jnp.concatenate(second, 1)


def put_back(ref, n, first, second):
    for s in range(8):
        a, b = first[:, 128 * s : 128 * (s + 1)], second[:, 128 * s : 128 * (s + 1)]
        low = low_lanes(a.shape)
        ref[s, n] = jnp.where(low, a, turned(b)).astype(BF16)
        ref[s + 8, n] = jnp.where(low, turned(a), b).astype(BF16)


def pack_kernel(q_ref, k_ref, v_ref, g_ref, w_hbm, out_ref, w_ref, sem):
    fetch = pltpu.make_async_copy(w_hbm, w_ref, sem)
    fetch.start()

    def place(n, rows):
        turned_rows = rows.T
        for slot in range(HEADS):
            at = HEAD_DIM * head_of(slot)
            out_ref[slot, n] = turned_rows[at : at + HEAD_DIM].astype(BF16)

    features = q_ref.shape[-1]
    for n, ref in enumerate((q_ref, k_ref, v_ref)):
        place(n, ref[...].reshape(-1, features))
    fetch.wait()
    place(
        3,
        jnp.dot(g_ref[...].reshape(-1, features), w_ref[...], preferred_element_type=F32).astype(BF16),
    )


def pack(query, key, value, upstream, weight):
    tokens = query.shape[0] * query.shape[1]
    return pl.pallas_call(
        pack_kernel,
        in_specs=[pl.BlockSpec(memory_space=pltpu.VMEM)] * 4 + [pl.BlockSpec(memory_space=pl.ANY)],
        out_specs=pl.BlockSpec(memory_space=pltpu.VMEM),
        out_shape=jax.ShapeDtypeStruct((HEADS, 4, HEAD_DIM, tokens), BF16),
        scratch_shapes=[pltpu.VMEM(weight.shape, BF16), pltpu.SemaphoreType.DMA],
        cost_estimate=pl.CostEstimate(flops=2 * tokens * weight.size, bytes_accessed=10_000_000, transcendentals=0),
        name="pack_by_head",
    )(query, key, value, upstream, weight)


def forward_kernel(x_ref, att_ref, e_ref, inv_ref, o_ref):
    qs, ks, vs = (frame_pair(x_ref, n) for n in range(3))
    for f in range(2):
        q_t, k, v_t = qs[f], ks[f].T, vs[f]
        for b in range(1024 // BLOCK):
            cols = slice(b * BLOCK, (b + 1) * BLOCK)
            scores = jnp.dot(k, q_t[:, cols], preferred_element_type=F32)
            row_max = jnp.max(scores, axis=0, keepdims=True)
            raised = jnp.exp2(scores * EXP2_SCALE - row_max * EXP2_SCALE)
            inverse = 1.0 / jnp.sum(raised, axis=0, keepdims=True)
            raised = raised.astype(BF16)
            e_ref[f, :, cols] = raised
            o_ref[f, :, cols] = jnp.dot(v_t, raised, preferred_element_type=F32) * inverse
            inv_ref[f, :, cols] = jnp.broadcast_to(inverse, (8, BLOCK))
    put_back(att_ref, 0, o_ref[0], o_ref[1])


PAIR = pl.BlockSpec((HEADS, 4, HEAD_DIM, 128), lambda i: (0, 0, 0, i))
ONE = pl.BlockSpec((HEADS, 1, HEAD_DIM, 128), lambda i: (0, 0, 0, i))
RAISED = pl.BlockSpec((2, 1024, 1024), lambda i: (i, 0, 0))
INVERSE = pl.BlockSpec((2, 8, 1024), lambda i: (i, 0, 0))


def forward(x):
    return pl.pallas_call(
        forward_kernel,
        grid=(2,),
        in_specs=[PAIR],
        out_specs=[ONE, RAISED, INVERSE],
        out_shape=[
            jax.ShapeDtypeStruct((HEADS, 1, HEAD_DIM, 256), BF16),
            jax.ShapeDtypeStruct((4, 1024, 1024), BF16),
            jax.ShapeDtypeStruct((4, 8, 1024), F32),
        ],
        scratch_shapes=[pltpu.VMEM((2, HEAD_DIM, 1024), F32)],
        cost_estimate=pl.CostEstimate(flops=4 * 4 * 1024 * 1024 * 256, bytes_accessed=12_000_000, transcendentals=1 << 22),
        name="spatial_forward",
    )(x)


def backward_kernel(x_ref, att_ref, e_ref, inv_ref, out_ref, dq_ref, dk_ref, dv_ref):
    qs, ks, vs, gs = (frame_pair(x_ref, n) for n in range(4))
    os = frame_pair(att_ref, 0)
    for f in range(2):
        q_t, k_t, v = qs[f], ks[f], vs[f].T
        scaled = gs[f].astype(F32) * inv_ref[f, 0:1, :]
        row_dot = jnp.sum(scaled * os[f].astype(F32), axis=0, keepdims=True)
        g_t = scaled.astype(BF16)
        for b in range(1024 // BLOCK):
            cols = slice(b * BLOCK, (b + 1) * BLOCK)
            raised = e_ref[f, :, cols]
            grad_probs = jnp.dot(v, g_t[:, cols], preferred_element_type=F32)
            grad_scores = (raised.astype(F32) * (grad_probs - row_dot[:, cols])).astype(BF16)
            dq_ref[f, :, cols] = jnp.dot(k_t, grad_scores, preferred_element_type=F32) * SOFTMAX_SCALE
            dk = lax.dot_general(q_t[:, cols], grad_scores, (((1,), (1,)), ((), ())), preferred_element_type=F32)
            dv = lax.dot_general(g_t[:, cols], raised, (((1,), (1,)), ((), ())), preferred_element_type=F32)
            if b == 0:
                dk_ref[f], dv_ref[f] = dk, dv
            else:
                dk_ref[f] += dk
                dv_ref[f] += dv
    put_back(out_ref, 0, dq_ref[0], dq_ref[1])
    put_back(out_ref, 1, dk_ref[0] * SOFTMAX_SCALE, dk_ref[1] * SOFTMAX_SCALE)
    put_back(out_ref, 2, dv_ref[0], dv_ref[1])


def backward(x, attended, raised, inverse):
    return pl.pallas_call(
        backward_kernel,
        grid=(2,),
        in_specs=[PAIR, ONE, RAISED, INVERSE],
        out_specs=pl.BlockSpec((HEADS, 3, HEAD_DIM, 128), lambda i: (0, 0, 0, i)),
        out_shape=jax.ShapeDtypeStruct((HEADS, 3, HEAD_DIM, 256), BF16),
        scratch_shapes=[pltpu.VMEM((2, HEAD_DIM, 1024), F32)] * 3,
        cost_estimate=pl.CostEstimate(flops=8 * 4 * 1024 * 1024 * 256, bytes_accessed=14_000_000, transcendentals=0),
        name="spatial_backward",
    )(x, attended, raised, inverse)


def weight_kernel(place_ref, mine_ref, other_ref, att_ref, o0, o1, o2, o3, g_ref, a_ref):
    core, z = place_ref[0], place_ref[1]
    features = mine_ref.shape[-1]
    g_ref[:, :256] = mine_ref[...].reshape(-1, features).T
    g_ref[:, 256:] = other_ref[...].reshape(-1, features).T
    for i in range(8):
        rows = slice(HEAD_DIM * i, HEAD_DIM * (i + 1))
        a_ref[rows, :256] = att_ref[i, core]
        a_ref[rows, 256:] = att_ref[i, 1 - core]
    att = a_ref[...]
    for r, out in enumerate((o0, o1, o2, o3)):
        for half in range(2):
            block = half * 4 + lax.rem(z + r, 4)
            rows = pl.ds(pl.multiple_of(block * 176, 16), 176)
            out[half] = lax.dot_general(
                g_ref[rows, :], att, (((1,), (1,)), ((), ())), preferred_element_type=F32
            ).astype(out.dtype)


def weight_terms(place, mine, other, att):
    features = mine.shape[-1]
    return pl.pallas_call(
        weight_kernel,
        in_specs=[pl.BlockSpec(memory_space=pltpu.SMEM)] + [pl.BlockSpec(memory_space=pltpu.VMEM)] * 3,
        out_specs=[pl.BlockSpec(memory_space=pltpu.VMEM)] * 4,
        out_shape=[jax.ShapeDtypeStruct((2, 176, 704), BF16)] * 4,
        scratch_shapes=[pltpu.VMEM((features, 512), BF16), pltpu.VMEM((704, 512), BF16)],
        cost_estimate=pl.CostEstimate(flops=2 * 512 * 1408 * 704, bytes_accessed=5_000_000, transcendentals=0),
        name="weight_terms",
    )(place, mine, other, att)


def rows_kernel(a, b, c, d, out):
    total = a[...].astype(F32) + b[...].astype(F32) + c[...].astype(F32) + d[...].astype(F32)
    total = total.reshape(352, 704)
    for p in range(32):
        out[p] = total[11 * p : 11 * (p + 1)].astype(BF16)


def row_sums(parts):
    return pl.pallas_call(
        rows_kernel,
        in_specs=[pl.BlockSpec(memory_space=pltpu.VMEM)] * 4,
        out_specs=pl.BlockSpec(memory_space=pltpu.VMEM),
        out_shape=jax.ShapeDtypeStruct((32, 11, 704), BF16),
        cost_estimate=pl.CostEstimate(flops=1_000_000, bytes_accessed=3_000_000, transcendentals=0),
        name="row_sums",
    )(*parts)


def unpack_kernel(x_ref, q_ref, k_ref, v_ref, t_ref):
    for n, ref in enumerate((q_ref, k_ref, v_ref)):
        for slot in range(HEADS):
            at = HEAD_DIM * head_of(slot)
            t_ref[at : at + HEAD_DIM] = x_ref[slot, n]
        ref[...] = t_ref[...].T.reshape(ref.shape)


def unpack(x, shape):
    return pl.pallas_call(
        unpack_kernel,
        in_specs=[pl.BlockSpec(memory_space=pltpu.VMEM)],
        out_specs=[pl.BlockSpec(memory_space=pltpu.VMEM)] * 3,
        out_shape=[jax.ShapeDtypeStruct(shape, BF16)] * 3,
        scratch_shapes=[pltpu.VMEM((shape[-1], shape[0] * shape[1]), BF16)],
        cost_estimate=pl.CostEstimate(flops=0, bytes_accessed=5_000_000, transcendentals=0),
        name="unpack_by_token",
    )(x)


FRAME, PATCH = ("y_lo", "z"), ("y_hi", "x", "core")
PLANE = ("y_lo", "y_hi", "x", "core")


def exchange(array, axes):
    return lax.all_to_all(array, axes, split_axis=0, concat_axis=0, tiled=True)


def along_z(array, step):
    return lax.ppermute(array, "z", [(i, (i + step) % 4) for i in range(4)])


def shards(query_rows, key_rows, value_rows, grad_out, out_weight):
    place = jnp.stack([lax.axis_index("core"), lax.axis_index("z")]).astype(jnp.int32)
    other_grad = lax.ppermute(grad_out, "core", [(0, 1), (1, 0)])
    x = exchange(pack(query_rows, key_rows, value_rows, grad_out, out_weight), PATCH)
    attended, raised, inverse = forward(x)
    att = exchange(attended.reshape(8, 2, HEAD_DIM, 256), ("y_hi", "x"))
    grads = backward(x, attended, raised, inverse)
    own, *sent = weight_terms(place, grad_out, other_grad, att)
    parts = [own] + [along_z(part, step + 1) for step, part in enumerate(sent)]
    home = exchange(grads, PATCH)
    rows = row_sums(parts)
    rows = exchange(rows, PLANE)
    outs = unpack(home, query_rows.shape)
    total = rows.reshape(16, 2, 11, 704).astype(F32).sum(0)
    grad_weight = jnp.concatenate([total[0], total[1]], axis=1)
    return (*outs, grad_weight)


def solution(mesh):
    chips = Mesh(mesh.devices.reshape(2, 4, 2, 4, 2), FRAME + PATCH)
    rows = P(FRAME, PATCH, None)
    return jax.shard_map(
        shards,
        mesh=chips,
        in_specs=(rows, rows, rows, rows, P()),
        out_specs=(rows, rows, rows, P(FRAME + PATCH, None)),
        check_vma=False,
    )
```

```python
import functools

import jax
import jax.numpy as jnp
from jax import lax
from jax.experimental import pallas as pl
from jax.experimental.pallas import tpu as pltpu
from jax.sharding import Mesh, PartitionSpec as P


HEAD_DIM = 88
HEADS = 16
HALF = 64
QUARTER = 22
PADDED = 24
BLOCK = 256
SOFTMAX_SCALE = HEAD_DIM ** (-0.5)
EXP2_SCALE = SOFTMAX_SCALE * 1.4426950408889634
F32, BF16 = jnp.float32, jnp.bfloat16


def head_of(slot):
    return 8 * (slot % 2) + slot // 2


def low_lanes(shape):
    return lax.broadcasted_iota(jnp.int32, shape, 1) < HALF


def turned(tile):
    return pltpu.roll(tile, HALF, 1)


def frame_pair(ref, n):
    first, second = [], []
    for s in range(8):
        a, b = ref[s, n].astype(F32), ref[s + 8, n].astype(F32)
        low = low_lanes(a.shape)
        first.append(jnp.where(low, a, turned(b)).astype(BF16))
        second.append(jnp.where(low, turned(a), b).astype(BF16))
    return jnp.concatenate(first, 1), jnp.concatenate(second, 1)


def put_back(ref, n, first, second):
    for s in range(8):
        a, b = first[:, 128 * s : 128 * (s + 1)], second[:, 128 * s : 128 * (s + 1)]
        low = low_lanes(a.shape)
        ref[s, n] = jnp.where(low, a, turned(b)).astype(BF16)
        ref[s + 8, n] = jnp.where(low, turned(a), b).astype(BF16)


def pack_kernel(q_ref, k_ref, v_ref, g_ref, w_hbm, out_ref, w_ref, sem):
    fetch = pltpu.make_async_copy(w_hbm, w_ref, sem)
    fetch.start()

    def place(n, rows):
        turned_rows = rows.T
        for slot in range(HEADS):
            at = HEAD_DIM * head_of(slot)
            out_ref[slot, n] = turned_rows[at : at + HEAD_DIM].astype(BF16)

    features = q_ref.shape[-1]
    for n, ref in enumerate((q_ref, k_ref, v_ref)):
        place(n, ref[...].reshape(-1, features))
    fetch.wait()
    place(
        3,
        jnp.dot(g_ref[...].reshape(-1, features), w_ref[...], preferred_element_type=F32).astype(BF16),
    )


def pack(query, key, value, upstream, weight):
    tokens = query.shape[0] * query.shape[1]
    return pl.pallas_call(
        pack_kernel,
        in_specs=[pl.BlockSpec(memory_space=pltpu.VMEM)] * 4 + [pl.BlockSpec(memory_space=pl.ANY)],
        out_specs=pl.BlockSpec(memory_space=pltpu.VMEM),
        out_shape=jax.ShapeDtypeStruct((HEADS, 4, HEAD_DIM, tokens), BF16),
        scratch_shapes=[pltpu.VMEM(weight.shape, BF16), pltpu.SemaphoreType.DMA],
        cost_estimate=pl.CostEstimate(flops=2 * tokens * weight.size, bytes_accessed=10_000_000, transcendentals=0),
        compiler_params=pltpu.CompilerParams(vmem_limit_bytes=62 << 20),
        name="pack_by_head",
    )(query, key, value, upstream, weight)


def forward_kernel(x_ref, att_ref, e_ref, row_ref, o_ref):
    qs, ks, vs, gs = (frame_pair(x_ref, n) for n in range(4))
    for f in range(2):
        q_t, k, v_t = qs[f], ks[f].T, vs[f]
        for b in range(1024 // BLOCK):
            cols = slice(b * BLOCK, (b + 1) * BLOCK)
            scores = jnp.dot(k, q_t[:, cols], preferred_element_type=F32)
            row_max = jnp.max(scores, axis=0, keepdims=True)
            raised = jnp.exp2(scores * EXP2_SCALE - row_max * EXP2_SCALE)
            inverse = 1.0 / jnp.sum(raised, axis=0, keepdims=True)
            raised = raised.astype(BF16)
            e_ref[f, :, cols] = raised
            attended = jnp.dot(v_t, raised, preferred_element_type=F32) * inverse
            o_ref[f, :, cols] = attended
            row_dot = jnp.sum(gs[f][:, cols].astype(F32) * attended, axis=0, keepdims=True) * inverse
            row_ref[f, 0:1, cols] = inverse
            row_ref[f, 1:2, cols] = row_dot
    for s in range(8):
        a, b = o_ref[0, :, 128 * s : 128 * (s + 1)], o_ref[1, :, 128 * s : 128 * (s + 1)]
        low = low_lanes(a.shape)
        for slot, tile in ((s, jnp.where(low, a, turned(b))), (s + 8, jnp.where(low, turned(a), b))):
            for quarter in range(4):
                rows = tile[QUARTER * quarter : QUARTER * (quarter + 1)]
                rows = jnp.concatenate([rows, jnp.zeros((PADDED - QUARTER, 128), F32)], axis=0)
                att_ref[quarter, slot // 2, slot % 2] = rows.astype(BF16)


PAIR = pl.BlockSpec((HEADS, 4, HEAD_DIM, 128), lambda i: (0, 0, 0, i))
RAISED = pl.BlockSpec((2, 1024, 1024), lambda i: (i, 0, 0))
PER_ROW = pl.BlockSpec((2, 8, 1024), lambda i: (i, 0, 0))


def forward(x):
    return pl.pallas_call(
        forward_kernel,
        grid=(2,),
        in_specs=[PAIR],
        out_specs=[pl.BlockSpec((4, 8, 2, PADDED, 128), lambda i: (0, 0, 0, 0, i)), RAISED, PER_ROW],
        out_shape=[
            jax.ShapeDtypeStruct((4, 8, 2, PADDED, 256), BF16),
            jax.ShapeDtypeStruct((4, 1024, 1024), BF16),
            jax.ShapeDtypeStruct((4, 8, 1024), F32),
        ],
        scratch_shapes=[pltpu.VMEM((2, HEAD_DIM, 1024), F32)],
        cost_estimate=pl.CostEstimate(flops=4 * 4 * 1024 * 1024 * 256, bytes_accessed=12_000_000, transcendentals=1 << 22),
        compiler_params=pltpu.CompilerParams(vmem_limit_bytes=60 << 20),
        name="spatial_forward",
    )(x)


def backward_kernel(x_ref, e_ref, row_ref, out_ref, dq_ref, dk_ref, dv_ref):
    qs, ks, vs, gs = (frame_pair(x_ref, n) for n in range(4))
    for f in range(2):
        q_t, k_t, v = qs[f], ks[f], vs[f].T
        g_t = (gs[f].astype(F32) * row_ref[f, 0:1, :]).astype(BF16)
        row_dot = row_ref[f, 1:2, :]
        for b in range(1024 // BLOCK):
            cols = slice(b * BLOCK, (b + 1) * BLOCK)
            raised = e_ref[f, :, cols]
            grad_probs = jnp.dot(v, g_t[:, cols], preferred_element_type=F32)
            grad_scores = (raised.astype(F32) * (grad_probs - row_dot[:, cols])).astype(BF16)
            dq_ref[f, :, cols] = jnp.dot(k_t, grad_scores, preferred_element_type=F32) * SOFTMAX_SCALE
            dk = lax.dot_general(q_t[:, cols], grad_scores, (((1,), (1,)), ((), ())), preferred_element_type=F32)
            dv = lax.dot_general(g_t[:, cols], raised, (((1,), (1,)), ((), ())), preferred_element_type=F32)
            if b == 0:
                dk_ref[f], dv_ref[f] = dk, dv
            else:
                dk_ref[f] += dk
                dv_ref[f] += dv
    put_back(out_ref, 0, dq_ref[0], dq_ref[1])
    put_back(out_ref, 1, dk_ref[0] * SOFTMAX_SCALE, dk_ref[1] * SOFTMAX_SCALE)
    put_back(out_ref, 2, dv_ref[0], dv_ref[1])


def backward(x, raised, per_row):
    return pl.pallas_call(
        backward_kernel,
        grid=(2,),
        in_specs=[PAIR, RAISED, PER_ROW],
        out_specs=pl.BlockSpec((HEADS, 3, HEAD_DIM, 128), lambda i: (0, 0, 0, i)),
        out_shape=jax.ShapeDtypeStruct((HEADS, 3, HEAD_DIM, 256), BF16),
        scratch_shapes=[pltpu.VMEM((2, HEAD_DIM, 1024), F32)] * 3,
        cost_estimate=pl.CostEstimate(flops=8 * 4 * 1024 * 1024 * 256, bytes_accessed=14_000_000, transcendentals=0),
        compiler_params=pltpu.CompilerParams(vmem_limit_bytes=60 << 20),
        name="spatial_backward",
    )(x, raised, per_row)


def weight_kernel(place_ref, *refs):
    grads, att_ref, outs, (a_ref, t_ref) = refs[:8], refs[8], refs[9:13], refs[13:]
    core, z, y = place_ref[0], place_ref[1], place_ref[2]
    total = None
    for r in range(4):
        source = lax.rem(z + 4 - r, 4)
        for side in range(2):
            spot = lax.rem(core + side, 2)
            for i in range(8):
                a_ref[QUARTER * i : QUARTER * (i + 1)] = att_ref[source * 8 + i, spot].astype(F32)[:QUARTER]
            grad = grads[4 * side + r][...]
            term = jnp.dot(
                a_ref[...].astype(BF16), grad.reshape(-1, grad.shape[-1]), preferred_element_type=F32
            )
            total = term if total is None else total + term
    t_ref[...] = total.T
    for s, out in enumerate(outs):
        to = lax.rem(y + s, 4)
        for depth in range(4):
            start = lax.rem(to, 2) * 704 + depth * 176 + (to // 2) * 88
            block = t_ref[pl.ds(pl.multiple_of(start, 8), 88), :]
            for x in range(4):
                out[x, depth] = block[QUARTER * x : QUARTER * (x + 1)].astype(out.dtype)


VM, SM = pl.BlockSpec(memory_space=pltpu.VMEM), pl.BlockSpec(memory_space=pltpu.SMEM)


def weight_terms(place, grads, att):
    shape = (4, 4, QUARTER, 8 * QUARTER)
    features = grads[0].shape[-1]
    return pl.pallas_call(
        weight_kernel,
        in_specs=[SM] + [VM] * 9,
        out_specs=[VM] * 4,
        out_shape=[jax.ShapeDtypeStruct(shape, F32)] + [jax.ShapeDtypeStruct(shape, BF16)] * 3,
        scratch_shapes=[pltpu.VMEM((8 * QUARTER, 256), F32), pltpu.VMEM((features, 8 * QUARTER), F32)],
        cost_estimate=pl.CostEstimate(flops=2 * 2048 * 1408 * 176, bytes_accessed=8_000_000, transcendentals=0),
        compiler_params=pltpu.CompilerParams(vmem_limit_bytes=24 << 20),
        name="weight_terms",
    )(place, *grads, att)


def sums_kernel(coordinate, place_ref, *refs):
    parts, outs, total = refs[:4], refs[4:8], refs[8]
    total[...] = sum(part[...].astype(F32) for part in parts[1:]) + parts[0][...]
    for s, out in enumerate(outs):
        out[...] = total[lax.rem(place_ref[coordinate] + s, 4)].astype(out.dtype)


def block_sums(place, parts, coordinate, sent):
    shape = parts[0].shape
    return pl.pallas_call(
        functools.partial(sums_kernel, coordinate),
        in_specs=[SM] + [VM] * 4,
        out_specs=[VM] * 4,
        out_shape=[jax.ShapeDtypeStruct(shape[1:], F32)] + [jax.ShapeDtypeStruct(shape[1:], sent)] * 3,
        scratch_shapes=[pltpu.VMEM(shape, F32)],
        cost_estimate=pl.CostEstimate(flops=1_000_000, bytes_accessed=3_000_000, transcendentals=0),
        compiler_params=pltpu.CompilerParams(vmem_limit_bytes=8 << 20),
        name="block_sums",
    )(place, *parts)


def pick_kernel(place_ref, *refs):
    parts, mine, theirs = refs[:4], refs[4], refs[5]
    core, z = place_ref[0], place_ref[1]
    for r, part in enumerate(parts):
        both = part[...]
        first, second = both[:11], both[11:]
        source = lax.rem(z + 4 - r, 4)
        mine[source] = jnp.where(core == 0, first, second)
        theirs[source] = jnp.where(core == 0, second, first)


def pick(place, parts):
    shape = jax.ShapeDtypeStruct((4, 11, 8 * QUARTER), F32)
    return pl.pallas_call(
        pick_kernel,
        in_specs=[SM] + [VM] * 4,
        out_specs=[VM] * 2,
        out_shape=[shape] * 2,
        cost_estimate=pl.CostEstimate(flops=1_000, bytes_accessed=200_000, transcendentals=0),
        compiler_params=pltpu.CompilerParams(vmem_limit_bytes=4 << 20),
        name="pick_rows",
    )(place, *parts)


def join_kernel(place_ref, mine, theirs, out, scratch):
    core = place_ref[0]
    scratch[core] = mine[...]
    scratch[1 - core] = theirs[...]
    for head in range(HEADS):
        i = head % 8
        for z in range(4):
            at = head * HEAD_DIM + z * QUARTER
            out[:, at : at + QUARTER] = scratch[head // 8, z][:, QUARTER * i : QUARTER * (i + 1)]


def join(place, mine, theirs):
    return pl.pallas_call(
        join_kernel,
        in_specs=[SM, VM, VM],
        out_specs=VM,
        out_shape=jax.ShapeDtypeStruct((11, HEADS * HEAD_DIM), F32),
        scratch_shapes=[pltpu.VMEM((2, 4, 11, 8 * QUARTER), F32)],
        cost_estimate=pl.CostEstimate(flops=1_000, bytes_accessed=200_000, transcendentals=0),
        compiler_params=pltpu.CompilerParams(vmem_limit_bytes=4 << 20),
        name="join_columns",
    )(place, mine, theirs)


def unpack_kernel(x_ref, q_ref, k_ref, v_ref, t_ref):
    for n, ref in enumerate((q_ref, k_ref, v_ref)):
        for slot in range(HEADS):
            at = HEAD_DIM * head_of(slot)
            t_ref[at : at + HEAD_DIM] = x_ref[slot, n]
        ref[...] = t_ref[...].T.reshape(ref.shape)


def unpack(x, shape):
    return pl.pallas_call(
        unpack_kernel,
        in_specs=[pl.BlockSpec(memory_space=pltpu.VMEM)],
        out_specs=[pl.BlockSpec(memory_space=pltpu.VMEM)] * 3,
        out_shape=[jax.ShapeDtypeStruct(shape, BF16)] * 3,
        scratch_shapes=[pltpu.VMEM((shape[-1], shape[0] * shape[1]), BF16)],
        cost_estimate=pl.CostEstimate(flops=0, bytes_accessed=5_000_000, transcendentals=0),
        compiler_params=pltpu.CompilerParams(vmem_limit_bytes=20 << 20),
        name="unpack_by_token",
    )(x)


FRAME, PATCH = ("y_lo", "z"), ("y_hi", "x", "core")


def exchange(array, axes):
    return lax.all_to_all(array, axes, split_axis=0, concat_axis=0, tiled=True)


def along(array, axis, step):
    return lax.ppermute(array, axis, [(i, (i + step) % 4) for i in range(4)])


def along_y(array, step):
    place = lambda y: (y % 2) * 2 + y // 2
    return lax.ppermute(array, ("y_lo", "y_hi"), [(place(y), place((y + step) % 4)) for y in range(4)])


def other_core(array):
    return lax.ppermute(array, "core", [(0, 1), (1, 0)])


def shards(query_rows, key_rows, value_rows, grad_out, out_weight):
    axis = lax.axis_index
    place = jnp.stack([axis("core"), axis("z"), axis("y_hi") * 2 + axis("y_lo"), axis("x")]).astype(jnp.int32)
    x = exchange(pack(query_rows, key_rows, value_rows, grad_out, out_weight), PATCH)
    gathered = [grad_out] + [along(grad_out, "z", r) for r in (1, 2, 3)]
    gathered += [other_core(array) for array in gathered]
    attended, raised, per_row = forward(x)
    att = exchange(attended.reshape(32, 2, PADDED, 256), ("z", "y_hi", "x"))
    grads = backward(x, raised, per_row)
    home = exchange(grads, PATCH)
    own, *sent = weight_terms(place, gathered, att)
    parts = [own] + [along_y(part, s) for s, part in enumerate(sent, 1)]
    own, *sent = block_sums(place, parts, 3, BF16)
    parts = [own] + [along(part, "x", s) for s, part in enumerate(sent, 1)]
    own, *sent = block_sums(place, parts, 1, F32)
    parts = [own] + [along(part, "z", s) for s, part in enumerate(sent, 1)]
    mine, theirs = pick(place, parts)
    theirs = other_core(theirs)
    grad_weight = join(place, mine, theirs)
    outs = unpack(home, query_rows.shape)
    return (*outs, grad_weight)


def solution(mesh):
    chips = Mesh(mesh.devices.reshape(2, 4, 2, 4, 2), FRAME + PATCH)
    rows = P(FRAME, PATCH, None)
    return jax.shard_map(
        shards,
        mesh=chips,
        in_specs=(rows, rows, rows, rows, P()),
        out_specs=(rows, rows, rows, P(FRAME + PATCH, None)),
        check_vma=False,
    )
```

```python
import jax
import jax.numpy as jnp
from jax import lax
from jax.experimental import pallas as pl
from jax.experimental.pallas import tpu as pltpu
from jax.sharding import Mesh, PartitionSpec as P


HEAD_DIM = 88
HEADS = 16
HALF = 64
QUARTER = 22
PADDED = 24
BLOCK = 256
SOFTMAX_SCALE = HEAD_DIM ** (-0.5)
EXP2_SCALE = SOFTMAX_SCALE * 1.4426950408889634
F32, BF16 = jnp.float32, jnp.bfloat16


def head_of(slot):
    return 8 * (slot % 2) + slot // 2


def low_lanes(shape):
    return lax.broadcasted_iota(jnp.int32, shape, 1) < HALF


def turned(tile):
    return pltpu.roll(tile, HALF, 1)


def frame_pair(ref, n):
    first, second = [], []
    for s in range(8):
        a, b = ref[s, n].astype(F32), ref[s + 8, n].astype(F32)
        low = low_lanes(a.shape)
        first.append(jnp.where(low, a, turned(b)).astype(BF16))
        second.append(jnp.where(low, turned(a), b).astype(BF16))
    return jnp.concatenate(first, 1), jnp.concatenate(second, 1)


def put_back(ref, n, first, second):
    for s in range(8):
        a, b = first[:, 128 * s : 128 * (s + 1)], second[:, 128 * s : 128 * (s + 1)]
        low = low_lanes(a.shape)
        ref[s, n] = jnp.where(low, a, turned(b)).astype(BF16)
        ref[s + 8, n] = jnp.where(low, turned(a), b).astype(BF16)


def pack_kernel(q_ref, k_ref, v_ref, g_ref, w_hbm, out_ref, w_ref, sem):
    fetch = pltpu.make_async_copy(w_hbm, w_ref, sem)
    fetch.start()

    def place(n, rows):
        turned_rows = rows.T
        for slot in range(HEADS):
            at = HEAD_DIM * head_of(slot)
            out_ref[slot, n] = turned_rows[at : at + HEAD_DIM].astype(BF16)

    features = q_ref.shape[-1]
    for n, ref in enumerate((q_ref, k_ref, v_ref)):
        place(n, ref[...].reshape(-1, features))
    fetch.wait()
    place(
        3,
        jnp.dot(g_ref[...].reshape(-1, features), w_ref[...], preferred_element_type=F32).astype(BF16),
    )


def pack(query, key, value, upstream, weight):
    tokens = query.shape[0] * query.shape[1]
    return pl.pallas_call(
        pack_kernel,
        in_specs=[pl.BlockSpec(memory_space=pltpu.VMEM)] * 4 + [pl.BlockSpec(memory_space=pl.ANY)],
        out_specs=pl.BlockSpec(memory_space=pltpu.VMEM),
        out_shape=jax.ShapeDtypeStruct((HEADS, 4, HEAD_DIM, tokens), BF16),
        scratch_shapes=[pltpu.VMEM(weight.shape, BF16), pltpu.SemaphoreType.DMA],
        cost_estimate=pl.CostEstimate(flops=2 * tokens * weight.size, bytes_accessed=10_000_000, transcendentals=0),
        compiler_params=pltpu.CompilerParams(vmem_limit_bytes=62 << 20),
        name="pack_by_head",
    )(query, key, value, upstream, weight)


def forward_kernel(x_ref, att_ref, e_ref, row_ref, o_ref):
    qs, ks, vs, gs = (frame_pair(x_ref, n) for n in range(4))
    for f in range(2):
        q_t, k, v_t = qs[f], ks[f].T, vs[f]
        for b in range(1024 // BLOCK):
            cols = slice(b * BLOCK, (b + 1) * BLOCK)
            scores = jnp.dot(k, q_t[:, cols], preferred_element_type=F32)
            row_max = jnp.max(scores, axis=0, keepdims=True)
            raised = jnp.exp2(scores * EXP2_SCALE - row_max * EXP2_SCALE)
            inverse = 1.0 / jnp.sum(raised, axis=0, keepdims=True)
            raised = raised.astype(BF16)
            e_ref[f, :, cols] = raised
            attended = jnp.dot(v_t, raised, preferred_element_type=F32) * inverse
            o_ref[f, :, cols] = attended
            row_dot = jnp.sum(gs[f][:, cols].astype(F32) * attended, axis=0, keepdims=True) * inverse
            row_ref[f, 0:1, cols] = inverse
            row_ref[f, 1:2, cols] = row_dot
    for s in range(8):
        a, b = o_ref[0, :, 128 * s : 128 * (s + 1)], o_ref[1, :, 128 * s : 128 * (s + 1)]
        low = low_lanes(a.shape)
        for slot, tile in ((s, jnp.where(low, a, turned(b))), (s + 8, jnp.where(low, turned(a), b))):
            for quarter in range(4):
                rows = tile[QUARTER * quarter : QUARTER * (quarter + 1)]
                rows = jnp.concatenate([rows, jnp.zeros((PADDED - QUARTER, 128), F32)], axis=0)
                att_ref[quarter, slot // 2, slot % 2] = rows.astype(BF16)


PAIR = pl.BlockSpec((HEADS, 4, HEAD_DIM, 128), lambda i: (0, 0, 0, i))
RAISED = pl.BlockSpec((2, 1024, 1024), lambda i: (i, 0, 0))
PER_ROW = pl.BlockSpec((2, 8, 1024), lambda i: (i, 0, 0))


def forward(x):
    return pl.pallas_call(
        forward_kernel,
        grid=(2,),
        in_specs=[PAIR],
        out_specs=[pl.BlockSpec((4, 8, 2, PADDED, 128), lambda i: (0, 0, 0, 0, i)), RAISED, PER_ROW],
        out_shape=[
            jax.ShapeDtypeStruct((4, 8, 2, PADDED, 256), BF16),
            jax.ShapeDtypeStruct((4, 1024, 1024), BF16),
            jax.ShapeDtypeStruct((4, 8, 1024), F32),
        ],
        scratch_shapes=[pltpu.VMEM((2, HEAD_DIM, 1024), F32)],
        cost_estimate=pl.CostEstimate(flops=4 * 4 * 1024 * 1024 * 256, bytes_accessed=12_000_000, transcendentals=1 << 22),
        compiler_params=pltpu.CompilerParams(vmem_limit_bytes=56 << 20),
        name="spatial_forward",
    )(x)


def backward_kernel(x_ref, e_ref, row_ref, out_ref, dq_ref, dk_ref, dv_ref):
    qs, ks, vs, gs = (frame_pair(x_ref, n) for n in range(4))
    for f in range(2):
        q_t, k_t, v = qs[f], ks[f], vs[f].T
        g_t = (gs[f].astype(F32) * row_ref[f, 0:1, :]).astype(BF16)
        row_dot = row_ref[f, 1:2, :]
        for b in range(1024 // BLOCK):
            cols = slice(b * BLOCK, (b + 1) * BLOCK)
            raised = e_ref[f, :, cols]
            grad_probs = jnp.dot(v, g_t[:, cols], preferred_element_type=F32)
            grad_scores = (raised.astype(F32) * (grad_probs - row_dot[:, cols])).astype(BF16)
            dq_ref[f, :, cols] = jnp.dot(k_t, grad_scores, preferred_element_type=F32) * SOFTMAX_SCALE
            dk = lax.dot_general(q_t[:, cols], grad_scores, (((1,), (1,)), ((), ())), preferred_element_type=F32)
            dv = lax.dot_general(g_t[:, cols], raised, (((1,), (1,)), ((), ())), preferred_element_type=F32)
            if b == 0:
                dk_ref[f], dv_ref[f] = dk, dv
            else:
                dk_ref[f] += dk
                dv_ref[f] += dv
    put_back(out_ref, 0, dq_ref[0], dq_ref[1])
    put_back(out_ref, 1, dk_ref[0] * SOFTMAX_SCALE, dk_ref[1] * SOFTMAX_SCALE)
    put_back(out_ref, 2, dv_ref[0], dv_ref[1])


def backward(x, raised, per_row):
    return pl.pallas_call(
        backward_kernel,
        grid=(2,),
        in_specs=[PAIR, RAISED, PER_ROW],
        out_specs=pl.BlockSpec((HEADS, 3, HEAD_DIM, 128), lambda i: (0, 0, 0, i)),
        out_shape=jax.ShapeDtypeStruct((HEADS, 3, HEAD_DIM, 256), BF16),
        scratch_shapes=[pltpu.VMEM((2, HEAD_DIM, 1024), F32)] * 3,
        cost_estimate=pl.CostEstimate(flops=8 * 4 * 1024 * 1024 * 256, bytes_accessed=14_000_000, transcendentals=0),
        compiler_params=pltpu.CompilerParams(vmem_limit_bytes=60 << 20),
        name="spatial_backward",
    )(x, raised, per_row)


def weight_kernel(place_ref, *refs):
    grads, att_ref, outs, (a_ref, t_ref) = refs[:8], refs[8], refs[9:13], refs[13:]
    core, z, y = place_ref[0], place_ref[1], place_ref[2]
    total = None
    for r in range(4):
        source = lax.rem(z + 4 - r, 4)
        for side in range(2):
            spot = lax.rem(core + side, 2)
            for i in range(8):
                a_ref[QUARTER * i : QUARTER * (i + 1)] = att_ref[source * 8 + i, spot].astype(F32)[:QUARTER]
            grad = grads[4 * side + r][...]
            term = jnp.dot(
                a_ref[...].astype(BF16), grad.reshape(-1, grad.shape[-1]), preferred_element_type=F32
            )
            total = term if total is None else total + term
    t_ref[...] = total.T
    for s, out in enumerate(outs):
        to = lax.rem(y + s, 4)
        for depth in range(4):
            start = lax.rem(to, 2) * 704 + depth * 176 + (to // 2) * 88
            block = t_ref[pl.ds(pl.multiple_of(start, 8), 88), :]
            for x in range(4):
                out[x, depth] = block[QUARTER * x : QUARTER * (x + 1)].astype(out.dtype)


VM, SM = pl.BlockSpec(memory_space=pltpu.VMEM), pl.BlockSpec(memory_space=pltpu.SMEM)


def weight_terms(place, grads, att):
    shape = (4, 4, QUARTER, 8 * QUARTER)
    features = grads[0].shape[-1]
    return pl.pallas_call(
        weight_kernel,
        in_specs=[SM] + [VM] * 9,
        out_specs=[VM] * 4,
        out_shape=[jax.ShapeDtypeStruct(shape, F32)] + [jax.ShapeDtypeStruct(shape, BF16)] * 3,
        scratch_shapes=[pltpu.VMEM((8 * QUARTER, 256), F32), pltpu.VMEM((features, 8 * QUARTER), F32)],
        cost_estimate=pl.CostEstimate(flops=2 * 2048 * 1408 * 176, bytes_accessed=8_000_000, transcendentals=0),
        compiler_params=pltpu.CompilerParams(vmem_limit_bytes=24 << 20),
        name="weight_terms",
    )(place, *grads, att)


def small(kernel, place, operands, shapes, scratch=()):
    return pl.pallas_call(
        kernel,
        in_specs=[SM] + [VM] * len(operands),
        out_specs=[VM] * len(shapes),
        out_shape=shapes,
        scratch_shapes=list(scratch),
        cost_estimate=pl.CostEstimate(flops=1_000_000, bytes_accessed=2_000_000, transcendentals=0),
        compiler_params=pltpu.CompilerParams(vmem_limit_bytes=8 << 20),
    )(place, *operands)


def sums_kernel(place_ref, *refs):
    parts, outs, total = refs[:4], refs[4:8], refs[8]
    for x in range(4):
        for z in range(4):
            total[z, x] = sum(part[x, z].astype(F32) for part in parts)
    for s, out in enumerate(outs):
        out[...] = total[lax.rem(place_ref[1] + s, 4)]


def pick_kernel(place_ref, *refs):
    parts, mine, theirs = refs[:4], refs[4], refs[5]
    core, z = place_ref[0], place_ref[1]
    for r, part in enumerate(parts):
        source = lax.rem(z + 4 - r, 4)
        for x in range(4):
            both = part[x]
            first, second = both[:11], both[11:]
            mine[source, x] = jnp.where(core == 0, first, second)
            theirs[source, x] = jnp.where(core == 0, second, first)


def join_kernel(place_ref, mine, theirs, *refs):
    outs, scratch, joined = refs[:4], refs[4], refs[5]
    core, place = place_ref[0], place_ref[3]
    scratch[core] = mine[...]
    scratch[1 - core] = theirs[...]
    for head in range(HEADS):
        i = head % 8
        for z in range(4):
            at = head * HEAD_DIM + z * QUARTER
            for x in range(4):
                joined[x, :, at : at + QUARTER] = scratch[head // 8, z, x][:, QUARTER * i : QUARTER * (i + 1)]
    for s, out in enumerate(outs):
        out[...] = joined[lax.rem(place + s, 4)].astype(out.dtype)


def final_kernel(place_ref, *refs):
    refs[4][...] = sum(part[...].astype(F32) for part in refs[:4])


def unpack_kernel(x_ref, q_ref, k_ref, v_ref, t_ref):
    for n, ref in enumerate((q_ref, k_ref, v_ref)):
        for slot in range(HEADS):
            at = HEAD_DIM * head_of(slot)
            t_ref[at : at + HEAD_DIM] = x_ref[slot, n]
        ref[...] = t_ref[...].T.reshape(ref.shape)


def unpack(x, shape):
    return pl.pallas_call(
        unpack_kernel,
        in_specs=[pl.BlockSpec(memory_space=pltpu.VMEM)],
        out_specs=[pl.BlockSpec(memory_space=pltpu.VMEM)] * 3,
        out_shape=[jax.ShapeDtypeStruct(shape, BF16)] * 3,
        scratch_shapes=[pltpu.VMEM((shape[-1], shape[0] * shape[1]), BF16)],
        cost_estimate=pl.CostEstimate(flops=0, bytes_accessed=5_000_000, transcendentals=0),
        compiler_params=pltpu.CompilerParams(vmem_limit_bytes=20 << 20),
        name="unpack_by_token",
    )(x)


FRAME, PATCH = ("y_lo", "z"), ("y_hi", "x", "core")


def exchange(array, axes):
    return lax.all_to_all(array, axes, split_axis=0, concat_axis=0, tiled=True)


def along(array, axis, step):
    return lax.ppermute(array, axis, [(i, (i + step) % 4) for i in range(4)])


def along_y(array, step):
    place = lambda y: (y % 2) * 2 + y // 2
    return lax.ppermute(array, ("y_lo", "y_hi"), [(place(y), place((y + step) % 4)) for y in range(4)])


def other_core(array):
    return lax.ppermute(array, "core", [(0, 1), (1, 0)])


def shards(query_rows, key_rows, value_rows, grad_out, out_weight):
    axis = lax.axis_index
    place = jnp.stack([axis("core"), axis("z"), axis("y_hi") * 2 + axis("y_lo"), axis("x")]).astype(jnp.int32)
    x = exchange(pack(query_rows, key_rows, value_rows, grad_out, out_weight), PATCH)
    gathered = [grad_out] + [along(grad_out, "z", r) for r in (1, 2, 3)]
    gathered += [other_core(array) for array in gathered]
    attended, raised, per_row = forward(x)
    att = exchange(attended.reshape(32, 2, PADDED, 256), ("z", "y_hi", "x"))
    grads = backward(x, raised, per_row)
    own, *sent = weight_terms(place, gathered, att)
    parts = [own] + [along_y(part, s) for s, part in enumerate(sent, 1)]
    home = exchange(grads, PATCH)
    columns, array = 8 * QUARTER, jax.ShapeDtypeStruct
    own, *sent = small(
        sums_kernel, place, parts, [array((4, QUARTER, columns), F32)] * 4, [pltpu.VMEM((4, 4, QUARTER, columns), F32)]
    )
    parts = [own] + [along(part, "z", s) for s, part in enumerate(sent, 1)]
    mine, theirs = small(pick_kernel, place, parts, [array((4, 4, 11, columns), F32)] * 2)
    theirs = other_core(theirs)
    features = grad_out.shape[-1]
    own, *sent = small(
        join_kernel,
        place,
        (mine, theirs),
        [array((11, features), F32)] + [array((11, features), BF16)] * 3,
        [pltpu.VMEM((2, 4, 4, 11, columns), F32), pltpu.VMEM((4, 11, features), F32)],
    )
    parts = [own] + [along(part, "x", s) for s, part in enumerate(sent, 1)]
    (grad_weight,) = small(final_kernel, place, parts, [array((11, features), F32)])
    outs = unpack(home, query_rows.shape)
    return (*outs, grad_weight)


def solution(mesh):
    chips = Mesh(mesh.devices.reshape(2, 4, 2, 4, 2), FRAME + PATCH)
    rows = P(FRAME, PATCH, None)
    return jax.shard_map(
        shards,
        mesh=chips,
        in_specs=(rows, rows, rows, rows, P()),
        out_specs=(rows, rows, rows, P(FRAME + PATCH, None)),
        check_vma=False,
    )
```

```python
import jax
import jax.numpy as jnp
from jax import lax
from jax.experimental import pallas as pl
from jax.experimental.pallas import tpu as pltpu
from jax.sharding import Mesh, PartitionSpec as P


HEAD_DIM = 88
HEADS = 16
HALF = 64
QUARTER = 22
PADDED = 24
BLOCK = 256
SOFTMAX_SCALE = HEAD_DIM ** (-0.5)
EXP2_SCALE = SOFTMAX_SCALE * 1.4426950408889634
F32, BF16 = jnp.float32, jnp.bfloat16


def head_of(slot):
    return 8 * (slot % 2) + slot // 2


def low_lanes(shape):
    return lax.broadcasted_iota(jnp.int32, shape, 1) < HALF


def turned(tile):
    return pltpu.roll(tile, HALF, 1)


def frame_pair(ref, n):
    first, second = [], []
    for s in range(8):
        a, b = ref[s, n].astype(F32), ref[s + 8, n].astype(F32)
        low = low_lanes(a.shape)
        first.append(jnp.where(low, a, turned(b)).astype(BF16))
        second.append(jnp.where(low, turned(a), b).astype(BF16))
    return jnp.concatenate(first, 1), jnp.concatenate(second, 1)


def put_back(ref, n, first, second):
    for s in range(8):
        a, b = first[:, 128 * s : 128 * (s + 1)], second[:, 128 * s : 128 * (s + 1)]
        low = low_lanes(a.shape)
        ref[s, n] = jnp.where(low, a, turned(b)).astype(BF16)
        ref[s + 8, n] = jnp.where(low, turned(a), b).astype(BF16)


def pack_kernel(*refs):
    ins, w_hbm, out_hbm, (in_ref, w_ref, out_ref, in_sem, w_sem, out_sem) = refs[:4], refs[4], refs[5], refs[6:]
    weight_load = pltpu.make_async_copy(w_hbm, w_ref, w_sem)
    loads = [pltpu.make_async_copy(ref, in_ref.at[n], in_sem.at[n]) for n, ref in enumerate(ins)]
    stores = [pltpu.make_async_copy(out_ref.at[n], out_hbm.at[:, n], out_sem.at[n]) for n in range(4)]
    for copy in (weight_load, *loads):
        copy.start()

    def rows_of(n):
        loads[n].wait()
        return in_ref[n].reshape(-1, in_ref.shape[-1])

    def place(n, rows):
        turned_rows = rows.T
        for slot in range(HEADS):
            at = HEAD_DIM * head_of(slot)
            out_ref[n, slot] = turned_rows[at : at + HEAD_DIM]
        stores[n].start()

    for n in range(3):
        place(n, rows_of(n))
    upstream = rows_of(3)
    weight_load.wait()
    place(3, jnp.dot(upstream, w_ref[...], preferred_element_type=F32).astype(BF16))
    for copy in stores:
        copy.wait()


def pack(query, key, value, upstream, weight):
    tokens = query.shape[0] * query.shape[1]
    hbm = pl.BlockSpec(memory_space=pl.ANY)
    dma = pltpu.SemaphoreType.DMA
    return pl.pallas_call(
        pack_kernel,
        in_specs=[hbm] * 5,
        out_specs=hbm,
        out_shape=jax.ShapeDtypeStruct((HEADS, 4, HEAD_DIM, tokens), BF16),
        scratch_shapes=[
            pltpu.VMEM((4, *query.shape), BF16),
            pltpu.VMEM(weight.shape, BF16),
            pltpu.VMEM((4, HEADS, HEAD_DIM, tokens), BF16),
            dma((4,)),
            dma,
            dma((4,)),
        ],
        cost_estimate=pl.CostEstimate(flops=2 * tokens * weight.size, bytes_accessed=10_000_000, transcendentals=0),
        compiler_params=pltpu.CompilerParams(vmem_limit_bytes=62 << 20),
        name="pack_by_head",
    )(query, key, value, upstream, weight)


def forward_kernel(x_ref, att_ref, e_ref, row_ref, o_ref):
    qs, ks, vs, gs = (frame_pair(x_ref, n) for n in range(4))
    for f in range(2):
        scores = jnp.dot(ks[f].T, qs[f], preferred_element_type=F32)
        row_max = jnp.max(scores, axis=0, keepdims=True)
        raised = jnp.exp2(scores * EXP2_SCALE - row_max * EXP2_SCALE)
        inverse = 1.0 / jnp.sum(raised, axis=0, keepdims=True)
        raised = raised.astype(BF16)
        e_ref[f] = raised
        attended = jnp.dot(vs[f], raised, preferred_element_type=F32) * inverse
        o_ref[f] = attended
        row_ref[f, 0:1] = inverse
        row_ref[f, 1:2] = jnp.sum(gs[f].astype(F32) * attended, axis=0, keepdims=True) * inverse
    for s in range(8):
        a, b = o_ref[0, :, 128 * s : 128 * (s + 1)], o_ref[1, :, 128 * s : 128 * (s + 1)]
        low = low_lanes(a.shape)
        for slot, tile in ((s, jnp.where(low, a, turned(b))), (s + 8, jnp.where(low, turned(a), b))):
            for quarter in range(4):
                rows = tile[QUARTER * quarter : QUARTER * (quarter + 1)]
                rows = jnp.concatenate([rows, jnp.zeros((PADDED - QUARTER, 128), F32)], axis=0)
                att_ref[quarter, slot // 2, slot % 2] = rows.astype(BF16)


PAIR = pl.BlockSpec((HEADS, 4, HEAD_DIM, 128), lambda i: (0, 0, 0, i))
RAISED = pl.BlockSpec((2, 1024, 1024), lambda i: (i, 0, 0))
PER_ROW = pl.BlockSpec((2, 8, 1024), lambda i: (i, 0, 0))


def forward(x):
    return pl.pallas_call(
        forward_kernel,
        grid=(2,),
        in_specs=[PAIR],
        out_specs=[pl.BlockSpec((4, 8, 2, PADDED, 128), lambda i: (0, 0, 0, 0, i)), RAISED, PER_ROW],
        out_shape=[
            jax.ShapeDtypeStruct((4, 8, 2, PADDED, 256), BF16),
            jax.ShapeDtypeStruct((4, 1024, 1024), BF16),
            jax.ShapeDtypeStruct((4, 8, 1024), F32),
        ],
        scratch_shapes=[pltpu.VMEM((2, HEAD_DIM, 1024), F32)],
        cost_estimate=pl.CostEstimate(flops=4 * 4 * 1024 * 1024 * 256, bytes_accessed=12_000_000, transcendentals=1 << 22),
        compiler_params=pltpu.CompilerParams(vmem_limit_bytes=56 << 20),
        name="spatial_forward",
    )(x)


def backward_kernel(x_ref, e_ref, row_ref, out_ref, dq_ref, dk_ref, dv_ref):
    qs, ks, vs, gs = (frame_pair(x_ref, n) for n in range(4))
    for f in range(2):
        q_t, k_t, v = qs[f], ks[f], vs[f].T
        g_t = (gs[f].astype(F32) * row_ref[f, 0:1, :]).astype(BF16)
        row_dot = row_ref[f, 1:2, :]
        for b in range(1024 // BLOCK):
            cols = slice(b * BLOCK, (b + 1) * BLOCK)
            raised = e_ref[f, :, cols]
            grad_probs = jnp.dot(v, g_t[:, cols], preferred_element_type=F32)
            grad_scores = (raised.astype(F32) * (grad_probs - row_dot[:, cols])).astype(BF16)
            dq_ref[f, :, cols] = jnp.dot(k_t, grad_scores, preferred_element_type=F32) * SOFTMAX_SCALE
            dk = lax.dot_general(q_t[:, cols], grad_scores, (((1,), (1,)), ((), ())), preferred_element_type=F32)
            dv = lax.dot_general(g_t[:, cols], raised, (((1,), (1,)), ((), ())), preferred_element_type=F32)
            if b == 0:
                dk_ref[f], dv_ref[f] = dk, dv
            else:
                dk_ref[f] += dk
                dv_ref[f] += dv
    put_back(out_ref, 0, dq_ref[0], dq_ref[1])
    put_back(out_ref, 1, dk_ref[0] * SOFTMAX_SCALE, dk_ref[1] * SOFTMAX_SCALE)
    put_back(out_ref, 2, dv_ref[0], dv_ref[1])


def backward(x, raised, per_row):
    return pl.pallas_call(
        backward_kernel,
        grid=(2,),
        in_specs=[PAIR, RAISED, PER_ROW],
        out_specs=pl.BlockSpec((HEADS, 3, HEAD_DIM, 128), lambda i: (0, 0, 0, i)),
        out_shape=jax.ShapeDtypeStruct((HEADS, 3, HEAD_DIM, 256), BF16),
        scratch_shapes=[pltpu.VMEM((2, HEAD_DIM, 1024), F32)] * 3,
        cost_estimate=pl.CostEstimate(flops=8 * 4 * 1024 * 1024 * 256, bytes_accessed=14_000_000, transcendentals=0),
        compiler_params=pltpu.CompilerParams(vmem_limit_bytes=60 << 20),
        name="spatial_backward",
    )(x, raised, per_row)


def weight_kernel(place_ref, *refs):
    grads, att_ref, outs, (a_ref, t_ref) = refs[:8], refs[8], refs[9:13], refs[13:]
    core, z, y = place_ref[0], place_ref[1], place_ref[2]
    total = None
    for r in range(4):
        source = lax.rem(z + 4 - r, 4)
        for side in range(2):
            spot = lax.rem(core + side, 2)
            for i in range(8):
                a_ref[QUARTER * i : QUARTER * (i + 1)] = att_ref[source * 8 + i, spot].astype(F32)[:QUARTER]
            grad = grads[4 * side + r][...]
            term = jnp.dot(
                a_ref[...].astype(BF16), grad.reshape(-1, grad.shape[-1]), preferred_element_type=F32
            )
            total = term if total is None else total + term
    t_ref[...] = total.T
    for s, out in enumerate(outs):
        to = lax.rem(y + s, 4)
        for depth in range(4):
            start = lax.rem(to, 2) * 704 + depth * 176 + (to // 2) * 88
            block = t_ref[pl.ds(pl.multiple_of(start, 8), 88), :]
            for x in range(4):
                out[x, depth] = block[QUARTER * x : QUARTER * (x + 1)].astype(out.dtype)


VM, SM = pl.BlockSpec(memory_space=pltpu.VMEM), pl.BlockSpec(memory_space=pltpu.SMEM)


def weight_terms(place, grads, att):
    shape = (4, 4, QUARTER, 8 * QUARTER)
    features = grads[0].shape[-1]
    return pl.pallas_call(
        weight_kernel,
        in_specs=[SM] + [VM] * 9,
        out_specs=[VM] * 4,
        out_shape=[jax.ShapeDtypeStruct(shape, F32)] + [jax.ShapeDtypeStruct(shape, BF16)] * 3,
        scratch_shapes=[pltpu.VMEM((8 * QUARTER, 256), F32), pltpu.VMEM((features, 8 * QUARTER), F32)],
        cost_estimate=pl.CostEstimate(flops=2 * 2048 * 1408 * 176, bytes_accessed=8_000_000, transcendentals=0),
        compiler_params=pltpu.CompilerParams(vmem_limit_bytes=24 << 20),
        name="weight_terms",
    )(place, *grads, att)


def small(kernel, place, operands, shapes, scratch=()):
    return pl.pallas_call(
        kernel,
        in_specs=[SM] + [VM] * len(operands),
        out_specs=[VM] * len(shapes),
        out_shape=shapes,
        scratch_shapes=list(scratch),
        cost_estimate=pl.CostEstimate(flops=1_000_000, bytes_accessed=2_000_000, transcendentals=0),
        compiler_params=pltpu.CompilerParams(vmem_limit_bytes=8 << 20),
    )(place, *operands)


def sums_kernel(place_ref, *refs):
    parts, outs, total = refs[:4], refs[4:8], refs[8]
    for x in range(4):
        for z in range(4):
            total[z, x] = sum(part[x, z].astype(F32) for part in parts)
    for s, out in enumerate(outs):
        out[...] = total[lax.rem(place_ref[1] + s, 4)]


def pick_kernel(place_ref, *refs):
    parts, mine, theirs = refs[:4], refs[4], refs[5]
    core, z = place_ref[0], place_ref[1]
    for r, part in enumerate(parts):
        source = lax.rem(z + 4 - r, 4)
        for x in range(4):
            both = part[x]
            first, second = both[:11], both[11:]
            mine[source, x] = jnp.where(core == 0, first, second)
            theirs[source, x] = jnp.where(core == 0, second, first)


def join_kernel(place_ref, mine, theirs, *refs):
    outs, scratch, joined = refs[:4], refs[4], refs[5]
    core, place = place_ref[0], place_ref[3]
    scratch[core] = mine[...]
    scratch[1 - core] = theirs[...]
    for head in range(HEADS):
        i = head % 8
        for z in range(4):
            at = head * HEAD_DIM + z * QUARTER
            for x in range(4):
                joined[x, :, at : at + QUARTER] = scratch[head // 8, z, x][:, QUARTER * i : QUARTER * (i + 1)]
    for s, out in enumerate(outs):
        out[...] = joined[lax.rem(place + s, 4)].astype(out.dtype)


def unpack_kernel(x_ref, *refs):
    parts, outs, total_ref, t_ref = refs[:4], refs[4:7], refs[7], refs[8]
    for n, ref in enumerate(outs):
        for slot in range(HEADS):
            at = HEAD_DIM * head_of(slot)
            t_ref[at : at + HEAD_DIM] = x_ref[slot, n]
        ref[...] = t_ref[...].T.reshape(ref.shape)
    total_ref[...] = sum(part[...].astype(F32) for part in parts)


def unpack(x, parts, shape):
    return pl.pallas_call(
        unpack_kernel,
        in_specs=[VM] * 5,
        out_specs=[VM] * 4,
        out_shape=[jax.ShapeDtypeStruct(shape, BF16)] * 3 + [jax.ShapeDtypeStruct(parts[0].shape, F32)],
        scratch_shapes=[pltpu.VMEM((shape[-1], shape[0] * shape[1]), BF16)],
        cost_estimate=pl.CostEstimate(flops=0, bytes_accessed=5_000_000, transcendentals=0),
        compiler_params=pltpu.CompilerParams(vmem_limit_bytes=20 << 20),
        name="unpack_by_token",
    )(x, *parts)


FRAME, PATCH = ("y_lo", "z"), ("y_hi", "x", "core")


def exchange(array, axes):
    return lax.all_to_all(array, axes, split_axis=0, concat_axis=0, tiled=True)


def along(array, axis, step):
    return lax.ppermute(array, axis, [(i, (i + step) % 4) for i in range(4)])


def along_y(array, step):
    place = lambda y: (y % 2) * 2 + y // 2
    return lax.ppermute(array, ("y_lo", "y_hi"), [(place(y), place((y + step) % 4)) for y in range(4)])


def other_core(array):
    return lax.ppermute(array, "core", [(0, 1), (1, 0)])


def shards(query_rows, key_rows, value_rows, grad_out, out_weight):
    axis = lax.axis_index
    place = jnp.stack([axis("core"), axis("z"), axis("y_hi") * 2 + axis("y_lo"), axis("x")]).astype(jnp.int32)
    x = exchange(pack(query_rows, key_rows, value_rows, grad_out, out_weight), PATCH)
    gathered = [grad_out] + [along(grad_out, "z", r) for r in (1, 2, 3)]
    gathered += [other_core(array) for array in gathered]
    attended, raised, per_row = forward(x)
    att = exchange(attended.reshape(32, 2, PADDED, 256), ("z", "y_hi", "x"))
    grads = backward(x, raised, per_row)
    own, *sent = weight_terms(place, gathered, att)
    parts = [own] + [along_y(part, s) for s, part in enumerate(sent, 1)]
    home = exchange(grads, PATCH)
    columns, array = 8 * QUARTER, jax.ShapeDtypeStruct
    own, *sent = small(
        sums_kernel, place, parts, [array((4, QUARTER, columns), F32)] * 4, [pltpu.VMEM((4, 4, QUARTER, columns), F32)]
    )
    parts = [own] + [along(part, "z", s) for s, part in enumerate(sent, 1)]
    mine, theirs = small(pick_kernel, place, parts, [array((4, 4, 11, columns), F32)] * 2)
    theirs = other_core(theirs)
    features = grad_out.shape[-1]
    own, *sent = small(
        join_kernel,
        place,
        (mine, theirs),
        [array((11, features), F32)] + [array((11, features), BF16)] * 3,
        [pltpu.VMEM((2, 4, 4, 11, columns), F32), pltpu.VMEM((4, 11, features), F32)],
    )
    parts = [own] + [along(part, "x", s) for s, part in enumerate(sent, 1)]
    *outs, grad_weight = unpack(home, parts, query_rows.shape)
    return (*outs, grad_weight)


def solution(mesh):
    chips = Mesh(mesh.devices.reshape(2, 4, 2, 4, 2), FRAME + PATCH)
    rows = P(FRAME, PATCH, None)
    return jax.shard_map(
        shards,
        mesh=chips,
        in_specs=(rows, rows, rows, rows, P()),
        out_specs=(rows, rows, rows, P(FRAME + PATCH, None)),
        check_vma=False,
    )
```

```python
import jax
import jax.numpy as jnp
from jax import lax
from jax.experimental import pallas as pl
from jax.experimental.pallas import tpu as pltpu
from jax.sharding import Mesh, PartitionSpec as P


HEAD_DIM = 88
HEADS = 16
HALF = 64
QUARTER = 22
PADDED = 24
PIECES = 8
BLOCK = 256
SOFTMAX_SCALE = HEAD_DIM ** (-0.5)
EXP2_SCALE = SOFTMAX_SCALE * 1.4426950408889634
F32, BF16 = jnp.float32, jnp.bfloat16


def head_of(slot):
    return 8 * (slot % 2) + slot // 2


def low_lanes(shape):
    return lax.broadcasted_iota(jnp.int32, shape, 1) < HALF


def turned(tile):
    return pltpu.roll(tile, HALF, 1)


def pair_lanes(pair):
    return slice(pair * 128, (pair + 1) * 128)


def frame_pair(ref, n, pair):
    first, second = [], []
    lanes = pair_lanes(pair)
    for s in range(8):
        a, b = ref[s, n, :, lanes].astype(F32), ref[s + 8, n, :, lanes].astype(F32)
        low = low_lanes(a.shape)
        first.append(jnp.where(low, a, turned(b)).astype(BF16))
        second.append(jnp.where(low, turned(a), b).astype(BF16))
    return jnp.concatenate(first, 1), jnp.concatenate(second, 1)


def put_back(ref, n, first, second):
    for s in range(8):
        a, b = first[:, 128 * s : 128 * (s + 1)], second[:, 128 * s : 128 * (s + 1)]
        low = low_lanes(a.shape)
        ref[s, n] = jnp.where(low, a, turned(b)).astype(BF16)
        ref[s + 8, n] = jnp.where(low, turned(a), b).astype(BF16)


def pack_kernel(*refs):
    ins, w_hbm, out_hbm, (in_ref, w_ref, out_ref, in_sem, w_sem, out_sem) = refs[:4], refs[4], refs[5], refs[6:]
    rows = w_ref.shape[0] // PIECES
    spans = [pl.ds(n * rows, rows) for n in range(PIECES)]
    weight_loads = [pltpu.make_async_copy(w_hbm.at[span], w_ref.at[span], w_sem.at[n]) for n, span in enumerate(spans)]
    loads = [pltpu.make_async_copy(ref, in_ref.at[n], in_sem.at[n]) for n, ref in enumerate(ins)]
    stores = [pltpu.make_async_copy(out_ref.at[n], out_hbm.at[:, n], out_sem.at[n]) for n in range(4)]
    for copy in (*loads, *weight_loads):
        copy.start()

    def rows_of(n):
        loads[n].wait()
        return in_ref[n].reshape(-1, in_ref.shape[-1])

    def place(n, rows):
        turned_rows = rows.T
        for slot in range(HEADS):
            at = HEAD_DIM * head_of(slot)
            out_ref[n, slot] = turned_rows[at : at + HEAD_DIM]
        stores[n].start()

    for n in range(3):
        place(n, rows_of(n))
    upstream = rows_of(3)
    for copy in weight_loads:
        copy.wait()
    place(3, jnp.dot(upstream, w_ref[...], preferred_element_type=F32).astype(BF16))
    for copy in stores:
        copy.wait()


def pack(query, key, value, upstream, weight):
    tokens = query.shape[0] * query.shape[1]
    hbm = pl.BlockSpec(memory_space=pl.ANY)
    dma = pltpu.SemaphoreType.DMA
    return pl.pallas_call(
        pack_kernel,
        in_specs=[hbm] * 5,
        out_specs=hbm,
        out_shape=jax.ShapeDtypeStruct((HEADS, 4, HEAD_DIM, tokens), BF16),
        scratch_shapes=[
            pltpu.VMEM((4, *query.shape), BF16),
            pltpu.VMEM(weight.shape, BF16),
            pltpu.VMEM((4, HEADS, HEAD_DIM, tokens), BF16),
            dma((4,)),
            dma((PIECES,)),
            dma((4,)),
        ],
        cost_estimate=pl.CostEstimate(flops=2 * tokens * weight.size, bytes_accessed=10_000_000, transcendentals=0),
        compiler_params=pltpu.CompilerParams(vmem_limit_bytes=62 << 20),
        name="pack_by_head",
    )(query, key, value, upstream, weight)


def stored(buffer, hbm, sem, pair):
    lead = (slice(None),) * (len(hbm.shape) - 1)
    return pltpu.make_async_copy(buffer.at[pair], hbm.at[(*lead, pair_lanes(pair))], sem.at[pair])


def forward_kernel(x_ref, att_hbm, e_hbm, row_ref, o_ref, att_ref, e_ref, sem, e_sem):
    def kept(frame):
        return pltpu.make_async_copy(e_ref.at[frame], e_hbm.at[frame], e_sem.at[frame])

    def step(pair, carry):
        qs, ks, vs, gs = (frame_pair(x_ref, n, pair) for n in range(4))
        for f in range(2):
            frame = 2 * pair + f
            scores = jnp.dot(ks[f].T, qs[f], preferred_element_type=F32)
            row_max = jnp.max(scores, axis=0, keepdims=True)
            raised = jnp.exp2(scores * EXP2_SCALE - row_max * EXP2_SCALE)
            inverse = 1.0 / jnp.sum(raised, axis=0, keepdims=True)
            raised = raised.astype(BF16)
            e_ref[frame] = raised
            kept(frame).start()
            attended = jnp.dot(vs[f], raised, preferred_element_type=F32) * inverse
            o_ref[f] = attended
            row_ref[frame, 0:1] = inverse
            row_ref[frame, 1:2] = jnp.sum(gs[f].astype(F32) * attended, axis=0, keepdims=True) * inverse
        for s in range(8):
            a, b = o_ref[0, :, 128 * s : 128 * (s + 1)], o_ref[1, :, 128 * s : 128 * (s + 1)]
            low = low_lanes(a.shape)
            for slot, tile in ((s, jnp.where(low, a, turned(b))), (s + 8, jnp.where(low, turned(a), b))):
                for quarter in range(4):
                    rows = tile[QUARTER * quarter : QUARTER * (quarter + 1)]
                    rows = jnp.concatenate([rows, jnp.zeros((PADDED - QUARTER, 128), F32)], axis=0)
                    att_ref[pair, quarter * 8 + slot // 2, slot % 2] = rows.astype(BF16)
        stored(att_ref, att_hbm, sem, pair).start()
        return carry

    for pair in range(2):
        step(pair, 0)
    for pair in range(2):
        stored(att_ref, att_hbm, sem, pair).wait()
    for frame in range(4):
        kept(frame).wait()


VM, SM = pl.BlockSpec(memory_space=pltpu.VMEM), pl.BlockSpec(memory_space=pltpu.SMEM)
HB = pl.BlockSpec(memory_space=pltpu.HBM)


def forward(x):
    return pl.pallas_call(
        forward_kernel,
        in_specs=[VM],
        out_specs=[HB, HB, VM],
        out_shape=[
            pltpu.HBM((32, 2, PADDED, 256), BF16),
            pltpu.HBM((4, 1024, 1024), BF16),
            jax.ShapeDtypeStruct((4, 8, 1024), F32),
        ],
        scratch_shapes=[
            pltpu.VMEM((2, HEAD_DIM, 1024), F32),
            pltpu.VMEM((2, 32, 2, PADDED, 128), BF16),
            pltpu.VMEM((4, 1024, 1024), BF16),
            pltpu.SemaphoreType.DMA((2,)),
            pltpu.SemaphoreType.DMA((4,)),
        ],
        cost_estimate=pl.CostEstimate(flops=4 * 4 * 1024 * 1024 * 256, bytes_accessed=12_000_000, transcendentals=1 << 22),
        compiler_params=pltpu.CompilerParams(vmem_limit_bytes=40 << 20),
        name="spatial_forward",
    )(x)


def backward_kernel(x_ref, e_ref, row_ref, out_ref, dq_ref, dk_ref, dv_ref):
    qs, ks, vs, gs = (frame_pair(x_ref, n, 0) for n in range(4))
    for f in range(2):
        q_t, k_t, v = qs[f], ks[f], vs[f].T
        g_t = (gs[f].astype(F32) * row_ref[f, 0:1, :]).astype(BF16)
        row_dot = row_ref[f, 1:2, :]
        for b in range(1024 // BLOCK):
            cols = slice(b * BLOCK, (b + 1) * BLOCK)
            raised = e_ref[f, :, cols]
            grad_probs = jnp.dot(v, g_t[:, cols], preferred_element_type=F32)
            grad_scores = (raised.astype(F32) * (grad_probs - row_dot[:, cols])).astype(BF16)
            dq_ref[f, :, cols] = jnp.dot(k_t, grad_scores, preferred_element_type=F32) * SOFTMAX_SCALE
            dk = lax.dot_general(q_t[:, cols], grad_scores, (((1,), (1,)), ((), ())), preferred_element_type=F32)
            dv = lax.dot_general(g_t[:, cols], raised, (((1,), (1,)), ((), ())), preferred_element_type=F32)
            if b == 0:
                dk_ref[f], dv_ref[f] = dk, dv
            else:
                dk_ref[f] += dk
                dv_ref[f] += dv
    put_back(out_ref, 0, dq_ref[0], dq_ref[1])
    put_back(out_ref, 1, dk_ref[0] * SOFTMAX_SCALE, dk_ref[1] * SOFTMAX_SCALE)
    put_back(out_ref, 2, dv_ref[0], dv_ref[1])


def backward(x, raised, per_row):
    return pl.pallas_call(
        backward_kernel,
        grid=(2,),
        in_specs=[
            pl.BlockSpec((HEADS, 4, HEAD_DIM, 128), lambda i: (0, 0, 0, i)),
            pl.BlockSpec((2, 1024, 1024), lambda i: (i, 0, 0)),
            pl.BlockSpec((2, 8, 1024), lambda i: (i, 0, 0)),
        ],
        out_specs=pl.BlockSpec((HEADS, 3, HEAD_DIM, 128), lambda i: (0, 0, 0, i)),
        out_shape=jax.ShapeDtypeStruct((HEADS, 3, HEAD_DIM, 256), BF16),
        scratch_shapes=[pltpu.VMEM((2, HEAD_DIM, 1024), F32)] * 3,
        cost_estimate=pl.CostEstimate(flops=8 * 4 * 1024 * 1024 * 256, bytes_accessed=14_000_000, transcendentals=0),
        compiler_params=pltpu.CompilerParams(vmem_limit_bytes=60 << 20),
        name="spatial_backward",
    )(x, raised, per_row)


def weight_kernel(place_ref, *refs):
    grads, att_ref, outs, (a_ref, t_ref) = refs[:8], refs[8], refs[9:13], refs[13:]
    core, z, y = place_ref[0], place_ref[1], place_ref[2]
    total = None
    for r in range(4):
        source = lax.rem(z + 4 - r, 4)
        for side in range(2):
            spot = lax.rem(core + side, 2)
            for i in range(8):
                a_ref[QUARTER * i : QUARTER * (i + 1)] = att_ref[source * 8 + i, spot].astype(F32)[:QUARTER]
            grad = grads[4 * side + r][...]
            term = jnp.dot(
                a_ref[...].astype(BF16), grad.reshape(-1, grad.shape[-1]), preferred_element_type=F32
            )
            total = term if total is None else total + term
    t_ref[...] = total.T
    for s, out in enumerate(outs):
        to = lax.rem(y + s, 4)
        for depth in range(4):
            start = lax.rem(to, 2) * 704 + depth * 176 + (to // 2) * 88
            block = t_ref[pl.ds(pl.multiple_of(start, 8), 88), :]
            for x in range(4):
                out[x, depth] = block[QUARTER * x : QUARTER * (x + 1)].astype(out.dtype)


def weight_terms(place, grads, att):
    shape = (4, 4, QUARTER, 8 * QUARTER)
    features = grads[0].shape[-1]
    return pl.pallas_call(
        weight_kernel,
        in_specs=[SM] + [VM] * 9,
        out_specs=[VM] * 4,
        out_shape=[jax.ShapeDtypeStruct(shape, F32)] + [jax.ShapeDtypeStruct(shape, BF16)] * 3,
        scratch_shapes=[pltpu.VMEM((8 * QUARTER, 256), F32), pltpu.VMEM((features, 8 * QUARTER), F32)],
        cost_estimate=pl.CostEstimate(flops=2 * 2048 * 1408 * 176, bytes_accessed=8_000_000, transcendentals=0),
        compiler_params=pltpu.CompilerParams(vmem_limit_bytes=24 << 20),
        name="weight_terms",
    )(place, *grads, att)


def small(kernel, place, operands, shapes, scratch=()):
    return pl.pallas_call(
        kernel,
        in_specs=[SM] + [VM] * len(operands),
        out_specs=[VM] * len(shapes),
        out_shape=shapes,
        scratch_shapes=list(scratch),
        cost_estimate=pl.CostEstimate(flops=1_000_000, bytes_accessed=2_000_000, transcendentals=0),
        compiler_params=pltpu.CompilerParams(vmem_limit_bytes=8 << 20),
    )(place, *operands)


def sums_kernel(place_ref, *refs):
    parts, outs, total = refs[:4], refs[4:8], refs[8]
    for x in range(4):
        for z in range(4):
            total[z, x] = sum(part[x, z].astype(F32) for part in parts)
    for s, out in enumerate(outs):
        out[...] = total[lax.rem(place_ref[1] + s, 4)]


def pick_kernel(place_ref, *refs):
    parts, mine, theirs = refs[:4], refs[4], refs[5]
    core, z = place_ref[0], place_ref[1]
    for r, part in enumerate(parts):
        source = lax.rem(z + 4 - r, 4)
        for x in range(4):
            both = part[x]
            first, second = both[:11], both[11:]
            mine[source, x] = jnp.where(core == 0, first, second)
            theirs[source, x] = jnp.where(core == 0, second, first)


def join_kernel(place_ref, mine, theirs, *refs):
    outs, scratch, joined = refs[:4], refs[4], refs[5]
    core, place = place_ref[0], place_ref[3]
    scratch[core] = mine[...]
    scratch[1 - core] = theirs[...]
    for head in range(HEADS):
        i = head % 8
        for z in range(4):
            at = head * HEAD_DIM + z * QUARTER
            for x in range(4):
                joined[x, :, at : at + QUARTER] = scratch[head // 8, z, x][:, QUARTER * i : QUARTER * (i + 1)]
    for s, out in enumerate(outs):
        out[...] = joined[lax.rem(place + s, 4)].astype(out.dtype)


def unpack_kernel(x_ref, *refs):
    parts, outs, total_ref, t_ref = refs[:4], refs[4:7], refs[7], refs[8]
    for n, ref in enumerate(outs):
        for slot in range(HEADS):
            at = HEAD_DIM * head_of(slot)
            t_ref[at : at + HEAD_DIM] = x_ref[slot, n]
        ref[...] = t_ref[...].T.reshape(ref.shape)
    total_ref[...] = sum(part[...].astype(F32) for part in parts)


def unpack(x, parts, shape):
    return pl.pallas_call(
        unpack_kernel,
        in_specs=[VM] * 5,
        out_specs=[VM] * 4,
        out_shape=[jax.ShapeDtypeStruct(shape, BF16)] * 3 + [jax.ShapeDtypeStruct(parts[0].shape, F32)],
        scratch_shapes=[pltpu.VMEM((shape[-1], shape[0] * shape[1]), BF16)],
        cost_estimate=pl.CostEstimate(flops=0, bytes_accessed=5_000_000, transcendentals=0),
        compiler_params=pltpu.CompilerParams(vmem_limit_bytes=20 << 20),
        name="unpack_by_token",
    )(x, *parts)


FRAME, PATCH = ("y_lo", "z"), ("y_hi", "x", "core")


def exchange(array, axes):
    return lax.all_to_all(array, axes, split_axis=0, concat_axis=0, tiled=True)


def along(array, axis, step):
    return lax.ppermute(array, axis, [(i, (i + step) % 4) for i in range(4)])


def along_y(array, step):
    place = lambda y: (y % 2) * 2 + y // 2
    return lax.ppermute(array, ("y_lo", "y_hi"), [(place(y), place((y + step) % 4)) for y in range(4)])


def other_core(array):
    return lax.ppermute(array, "core", [(0, 1), (1, 0)])


def shards(query_rows, key_rows, value_rows, grad_out, out_weight):
    axis = lax.axis_index
    place = jnp.stack([axis("core"), axis("z"), axis("y_hi") * 2 + axis("y_lo"), axis("x")]).astype(jnp.int32)
    x = exchange(pack(query_rows, key_rows, value_rows, grad_out, out_weight), PATCH)
    gathered = [grad_out] + [along(grad_out, "z", r) for r in (1, 2, 3)]
    gathered += [other_core(array) for array in gathered]
    attended, raised, per_row = forward(x)
    att = exchange(attended, ("z", "y_hi", "x"))
    grads = backward(x, raised, per_row)
    own, *sent = weight_terms(place, gathered, att)
    parts = [own] + [along_y(part, s) for s, part in enumerate(sent, 1)]
    home = exchange(grads, PATCH)
    columns, array = 8 * QUARTER, jax.ShapeDtypeStruct
    own, *sent = small(
        sums_kernel, place, parts, [array((4, QUARTER, columns), F32)] * 4, [pltpu.VMEM((4, 4, QUARTER, columns), F32)]
    )
    parts = [own] + [along(part, "z", s) for s, part in enumerate(sent, 1)]
    mine, theirs = small(pick_kernel, place, parts, [array((4, 4, 11, columns), F32)] * 2)
    theirs = other_core(theirs)
    features = grad_out.shape[-1]
    own, *sent = small(
        join_kernel,
        place,
        (mine, theirs),
        [array((11, features), F32)] + [array((11, features), BF16)] * 3,
        [pltpu.VMEM((2, 4, 4, 11, columns), F32), pltpu.VMEM((4, 11, features), F32)],
    )
    parts = [own] + [along(part, "x", s) for s, part in enumerate(sent, 1)]
    *outs, grad_weight = unpack(home, parts, query_rows.shape)
    return (*outs, grad_weight)


def solution(mesh):
    chips = Mesh(mesh.devices.reshape(2, 4, 2, 4, 2), FRAME + PATCH)
    rows = P(FRAME, PATCH, None)
    return jax.shard_map(
        shards,
        mesh=chips,
        in_specs=(rows, rows, rows, rows, P()),
        out_specs=(rows, rows, rows, P(FRAME + PATCH, None)),
        check_vma=False,
    )
```

```python
import jax
import jax.numpy as jnp
from jax import lax
from jax.experimental import pallas as pl
from jax.experimental.pallas import tpu as pltpu
from jax.sharding import Mesh, PartitionSpec as P


HEAD_DIM = 88
HEADS = 16
HALF = 64
QUARTER = 22
PADDED = 24
COLUMNS = 8 * PADDED
PIECES = 11
BLOCK = 256
SOFTMAX_SCALE = HEAD_DIM ** (-0.5)
EXP2_SCALE = SOFTMAX_SCALE * 1.4426950408889634
F32, BF16 = jnp.float32, jnp.bfloat16


def head_of(slot):
    return 8 * (slot % 2) + slot // 2


def low_lanes(shape):
    return lax.broadcasted_iota(jnp.int32, shape, 1) < HALF


def turned(tile):
    return pltpu.roll(tile, HALF, 1)


def pair_lanes(pair):
    return slice(pair * 128, (pair + 1) * 128)


def frame_pair(ref, n, pair):
    first, second = [], []
    lanes = pair_lanes(pair)
    for s in range(8):
        a, b = ref[s, n, :, lanes].astype(F32), ref[s + 8, n, :, lanes].astype(F32)
        low = low_lanes(a.shape)
        first.append(jnp.where(low, a, turned(b)).astype(BF16))
        second.append(jnp.where(low, turned(a), b).astype(BF16))
    return jnp.concatenate(first, 1), jnp.concatenate(second, 1)


def put_back(ref, n, first, second):
    for s in range(8):
        a, b = first[:, 128 * s : 128 * (s + 1)], second[:, 128 * s : 128 * (s + 1)]
        low = low_lanes(a.shape)
        ref[s, n] = jnp.where(low, a, turned(b)).astype(BF16)
        ref[s + 8, n] = jnp.where(low, turned(a), b).astype(BF16)


def pack_kernel(*refs):
    ins, w_hbm, out_hbm, (in_ref, w_ref, out_ref, in_sem, w_sem, out_sem) = refs[:4], refs[4], refs[5], refs[6:]
    rows = w_ref.shape[0] // PIECES
    spans = [pl.ds(n * rows, rows) for n in range(PIECES)]
    weight_loads = [pltpu.make_async_copy(w_hbm.at[span], w_ref.at[span], w_sem.at[n]) for n, span in enumerate(spans)]
    loads = [pltpu.make_async_copy(ref, in_ref.at[n], in_sem.at[n]) for n, ref in enumerate(ins)]
    stores = [pltpu.make_async_copy(out_ref.at[n], out_hbm.at[:, n], out_sem.at[n]) for n in range(4)]
    for copy in (*loads, *weight_loads):
        copy.start()

    def rows_of(n):
        loads[n].wait()
        return in_ref[n].reshape(-1, in_ref.shape[-1])

    def place(n, rows):
        turned_rows = rows.T
        for slot in range(HEADS):
            at = HEAD_DIM * head_of(slot)
            out_ref[n, slot] = turned_rows[at : at + HEAD_DIM]
        stores[n].start()

    for n in range(3):
        place(n, rows_of(n))
    upstream = rows_of(3)
    for copy in weight_loads:
        copy.wait()
    place(3, jnp.dot(upstream, w_ref[...], preferred_element_type=F32).astype(BF16))
    for copy in stores:
        copy.wait()


def pack(query, key, value, upstream, weight):
    tokens = query.shape[0] * query.shape[1]
    hbm = pl.BlockSpec(memory_space=pl.ANY)
    dma = pltpu.SemaphoreType.DMA
    return pl.pallas_call(
        pack_kernel,
        in_specs=[hbm] * 5,
        out_specs=hbm,
        out_shape=jax.ShapeDtypeStruct((HEADS, 4, HEAD_DIM, tokens), BF16),
        scratch_shapes=[
            pltpu.VMEM((4, *query.shape), BF16),
            pltpu.VMEM(weight.shape, BF16),
            pltpu.VMEM((4, HEADS, HEAD_DIM, tokens), BF16),
            dma((4,)),
            dma((PIECES,)),
            dma((4,)),
        ],
        cost_estimate=pl.CostEstimate(flops=2 * tokens * weight.size, bytes_accessed=10_000_000, transcendentals=0),
        compiler_params=pltpu.CompilerParams(vmem_limit_bytes=62 << 20),
        name="pack_by_head",
    )(query, key, value, upstream, weight)


def stored(buffer, hbm, sem, pair):
    lead = (slice(None),) * (len(hbm.shape) - 1)
    return pltpu.make_async_copy(buffer.at[pair], hbm.at[(*lead, pair_lanes(pair))], sem.at[pair])


def forward_kernel(x_ref, att_hbm, e_hbm, row_hbm, o_ref, att_ref, e_ref, row_ref, sem, e_sem, row_sem):
    row_copy = pltpu.make_async_copy(row_ref, row_hbm, row_sem)

    def kept(frame):
        return pltpu.make_async_copy(e_ref.at[frame], e_hbm.at[frame], e_sem.at[frame])

    def step(pair, carry):
        qs, ks, vs, gs = (frame_pair(x_ref, n, pair) for n in range(4))
        raw = [jnp.dot(ks[f].T, qs[f], preferred_element_type=F32) for f in range(2)]
        for f in range(2):
            frame = 2 * pair + f
            scores = raw[f]
            row_max = jnp.max(scores, axis=0, keepdims=True)
            raised = jnp.exp2(scores * EXP2_SCALE - row_max * EXP2_SCALE)
            inverse = 1.0 / jnp.sum(raised, axis=0, keepdims=True)
            raised = raised.astype(BF16)
            e_ref[frame] = raised
            kept(frame).start()
            attended = jnp.dot(vs[f], raised, preferred_element_type=F32) * inverse
            o_ref[f] = attended
            row_ref[frame, 0:1] = inverse
            row_ref[frame, 1:2] = jnp.sum(gs[f].astype(F32) * attended, axis=0, keepdims=True) * inverse
        if pair == 1:
            row_copy.start()
        for s in range(8):
            a, b = o_ref[0, :, 128 * s : 128 * (s + 1)], o_ref[1, :, 128 * s : 128 * (s + 1)]
            low = low_lanes(a.shape)
            for slot, tile in ((s, jnp.where(low, a, turned(b))), (s + 8, jnp.where(low, turned(a), b))):
                for quarter in range(4):
                    rows = tile[QUARTER * quarter : QUARTER * (quarter + 1)]
                    rows = jnp.concatenate([rows, jnp.zeros((PADDED - QUARTER, 128), F32)], axis=0)
                    att_ref[pair, quarter * 8 + slot // 2, slot % 2] = rows.astype(BF16)
        stored(att_ref, att_hbm, sem, pair).start()
        return carry

    for pair in range(2):
        step(pair, 0)
    for pair in range(2):
        stored(att_ref, att_hbm, sem, pair).wait()
    for frame in range(4):
        kept(frame).wait()
    row_copy.wait()


VM, SM = pl.BlockSpec(memory_space=pltpu.VMEM), pl.BlockSpec(memory_space=pltpu.SMEM)
HB = pl.BlockSpec(memory_space=pltpu.HBM)


def forward(x):
    return pl.pallas_call(
        forward_kernel,
        in_specs=[VM],
        out_specs=[HB, HB, HB],
        out_shape=[
            pltpu.HBM((32, 2, PADDED, 256), BF16),
            pltpu.HBM((4, 1024, 1024), BF16),
            pltpu.HBM((4, 8, 1024), F32),
        ],
        scratch_shapes=[
            pltpu.VMEM((2, HEAD_DIM, 1024), F32),
            pltpu.VMEM((2, 32, 2, PADDED, 128), BF16),
            pltpu.VMEM((4, 1024, 1024), BF16),
            pltpu.VMEM((4, 8, 1024), F32),
            pltpu.SemaphoreType.DMA((2,)),
            pltpu.SemaphoreType.DMA((4,)),
            pltpu.SemaphoreType.DMA,
        ],
        cost_estimate=pl.CostEstimate(flops=4 * 4 * 1024 * 1024 * 256, bytes_accessed=12_000_000, transcendentals=1 << 22),
        compiler_params=pltpu.CompilerParams(vmem_limit_bytes=40 << 20),
        name="spatial_forward",
    )(x)


def backward_kernel(x_ref, e_ref, row_ref, out_ref, dq_ref, dk_ref, dv_ref):
    qs, ks, vs, gs = (frame_pair(x_ref, n, 0) for n in range(4))
    for f in range(2):
        q_t, k_t, v = qs[f], ks[f], vs[f].T
        g_t = (gs[f].astype(F32) * row_ref[f, 0:1, :]).astype(BF16)
        row_dot = row_ref[f, 1:2, :]
        for b in range(1024 // BLOCK):
            cols = slice(b * BLOCK, (b + 1) * BLOCK)
            raised = e_ref[f, :, cols]
            grad_probs = jnp.dot(v, g_t[:, cols], preferred_element_type=F32)
            grad_scores = (raised.astype(F32) * (grad_probs - row_dot[:, cols])).astype(BF16)
            dq_ref[f, :, cols] = jnp.dot(k_t, grad_scores, preferred_element_type=F32) * SOFTMAX_SCALE
            dk = lax.dot_general(q_t[:, cols], grad_scores, (((1,), (1,)), ((), ())), preferred_element_type=F32)
            dv = lax.dot_general(g_t[:, cols], raised, (((1,), (1,)), ((), ())), preferred_element_type=F32)
            if b == 0:
                dk_ref[f], dv_ref[f] = dk, dv
            else:
                dk_ref[f] += dk
                dv_ref[f] += dv
    put_back(out_ref, 0, dq_ref[0], dq_ref[1])
    put_back(out_ref, 1, dk_ref[0] * SOFTMAX_SCALE, dk_ref[1] * SOFTMAX_SCALE)
    put_back(out_ref, 2, dv_ref[0], dv_ref[1])


def backward(x, raised, per_row):
    return pl.pallas_call(
        backward_kernel,
        grid=(2,),
        in_specs=[
            pl.BlockSpec((HEADS, 4, HEAD_DIM, 128), lambda i: (0, 0, 0, i)),
            pl.BlockSpec((2, 1024, 1024), lambda i: (i, 0, 0)),
            pl.BlockSpec((2, 8, 1024), lambda i: (i, 0, 0)),
        ],
        out_specs=pl.BlockSpec((HEADS, 3, HEAD_DIM, 128), lambda i: (0, 0, 0, i)),
        out_shape=jax.ShapeDtypeStruct((HEADS, 3, HEAD_DIM, 256), BF16),
        scratch_shapes=[pltpu.VMEM((2, HEAD_DIM, 1024), F32)] * 3,
        cost_estimate=pl.CostEstimate(flops=8 * 4 * 1024 * 1024 * 256, bytes_accessed=14_000_000, transcendentals=0),
        compiler_params=pltpu.CompilerParams(vmem_limit_bytes=60 << 20),
        name="spatial_backward",
    )(x, raised, per_row)


def in_hbm(array):
    return pltpu.with_memory_space_constraint(array, pltpu.HBM)


def weight_kernel(place_ref, *refs):
    grads, att_ref, outs, (g_ref, t_ref, sem) = refs[:8], refs[8], refs[9:13], refs[13:]
    core, z, y = place_ref[0], place_ref[1], place_ref[2]
    loads = [pltpu.make_async_copy(grads[n], g_ref.at[n], sem.at[n]) for n in range(8)]
    for copy in loads:
        copy.start()
    total = None
    for n in range(8):
        if n % 2 == 0:
            loads[n].wait()
            loads[n + 1].wait()
        source, spot = lax.rem(z + 4 - n % 4, 4), lax.rem(core + n // 4, 2)
        block = att_ref[pl.ds(source * 8, 8), spot].reshape(COLUMNS, 256)
        term = jnp.dot(block, g_ref[n].reshape(256, g_ref.shape[-1]), preferred_element_type=F32)
        total = term if total is None else total + term
    t_ref[...] = total.T
    for s, out in enumerate(outs):
        to = lax.rem(y + s, 4)
        for depth in range(4):
            start = lax.rem(to, 2) * 704 + depth * 176 + (to // 2) * 88
            block = t_ref[pl.ds(pl.multiple_of(start, 8), 88), :]
            for x in range(4):
                rows = block[QUARTER * x : QUARTER * (x + 1)].astype(out.dtype)
                out[depth, x // 2, :, COLUMNS * (x % 2) : COLUMNS * (x % 2 + 1)] = rows


def weight_terms(place, grads, att):
    shape = (4, 2, QUARTER, 2 * COLUMNS)
    return pl.pallas_call(
        weight_kernel,
        in_specs=[SM] + [HB] * 8 + [VM],
        out_specs=[VM] * 4,
        out_shape=[jax.ShapeDtypeStruct(shape, F32)] + [jax.ShapeDtypeStruct(shape, BF16)] * 3,
        scratch_shapes=[
            pltpu.VMEM((8, *grads[0].shape), BF16),
            pltpu.VMEM((grads[0].shape[-1], COLUMNS), F32),
            pltpu.SemaphoreType.DMA((8,)),
        ],
        cost_estimate=pl.CostEstimate(flops=2 * 2048 * 1408 * 176, bytes_accessed=8_000_000, transcendentals=0),
        compiler_params=pltpu.CompilerParams(vmem_limit_bytes=24 << 20),
        name="weight_terms",
    )(place, *map(in_hbm, grads), att)


def small(kernel, place, operands, shapes, scratch=()):
    return pl.pallas_call(
        kernel,
        in_specs=[SM] + [VM] * len(operands),
        out_specs=[VM] * len(shapes),
        out_shape=shapes,
        scratch_shapes=list(scratch),
        cost_estimate=pl.CostEstimate(flops=1_000_000, bytes_accessed=2_000_000, transcendentals=0),
        compiler_params=pltpu.CompilerParams(vmem_limit_bytes=8 << 20),
    )(place, *operands)


def sums_kernel(place_ref, *refs):
    parts, outs, total = refs[:4], refs[4:8], refs[8]
    for x in range(4):
        for z in range(4):
            columns = slice(COLUMNS * (x % 2), COLUMNS * (x % 2 + 1))
            total[z, x] = sum(part[z, x // 2, :, columns].astype(F32) for part in parts)
    for s, out in enumerate(outs):
        out[...] = total[lax.rem(place_ref[1] + s, 4)]


def pick_kernel(place_ref, *refs):
    parts, mine, theirs = refs[:4], refs[4], refs[5]
    core, z = place_ref[0], place_ref[1]
    for r, part in enumerate(parts):
        source = lax.rem(z + 4 - r, 4)
        for x in range(4):
            both = part[x]
            first, second = both[:11], both[11:]
            mine[source, x] = jnp.where(core == 0, first, second)
            theirs[source, x] = jnp.where(core == 0, second, first)


def join_kernel(place_ref, mine, theirs, *refs):
    outs, scratch, joined = refs[:4], refs[4], refs[5]
    core, place = place_ref[0], place_ref[3]
    scratch[core] = mine[...]
    scratch[1 - core] = theirs[...]
    for head in range(HEADS):
        i = head % 8
        for z in range(4):
            at = head * HEAD_DIM + z * QUARTER
            for x in range(4):
                joined[x, :, at : at + QUARTER] = scratch[head // 8, z, x][:, PADDED * i : PADDED * i + QUARTER]
    for s, out in enumerate(outs):
        out[...] = joined[lax.rem(place + s, 4)].astype(out.dtype)


def unpack_kernel(x_ref, *refs):
    parts, outs, total_ref, t_ref = refs[:4], refs[4:7], refs[7], refs[8]
    for n, ref in enumerate(outs):
        for slot in range(HEADS):
            at = HEAD_DIM * head_of(slot)
            t_ref[at : at + HEAD_DIM] = x_ref[slot, n]
        ref[...] = t_ref[...].T.reshape(ref.shape)
    total_ref[...] = sum(part[...].astype(F32) for part in parts)


def unpack(x, parts, shape):
    return pl.pallas_call(
        unpack_kernel,
        in_specs=[VM] * 5,
        out_specs=[VM] * 4,
        out_shape=[jax.ShapeDtypeStruct(shape, BF16)] * 3 + [jax.ShapeDtypeStruct(parts[0].shape, F32)],
        scratch_shapes=[pltpu.VMEM((shape[-1], shape[0] * shape[1]), BF16)],
        cost_estimate=pl.CostEstimate(flops=0, bytes_accessed=5_000_000, transcendentals=0),
        compiler_params=pltpu.CompilerParams(vmem_limit_bytes=20 << 20),
        name="unpack_by_token",
    )(x, *parts)


FRAME, PATCH = ("y_lo", "z"), ("y_hi", "x", "core")


def exchange(array, axes):
    return lax.all_to_all(array, axes, split_axis=0, concat_axis=0, tiled=True)


def along(array, axis, step):
    return lax.ppermute(array, axis, [(i, (i + step) % 4) for i in range(4)])


def along_y(array, step):
    place = lambda y: (y % 2) * 2 + y // 2
    return lax.ppermute(array, ("y_lo", "y_hi"), [(place(y), place((y + step) % 4)) for y in range(4)])


def other_core(array):
    return lax.ppermute(array, "core", [(0, 1), (1, 0)])


def shards(query_rows, key_rows, value_rows, grad_out, out_weight):
    axis = lax.axis_index
    place = jnp.stack([axis("core"), axis("z"), axis("y_hi") * 2 + axis("y_lo"), axis("x")]).astype(jnp.int32)
    x = exchange(pack(query_rows, key_rows, value_rows, grad_out, out_weight), PATCH)
    gathered = [grad_out] + [along(grad_out, "z", r) for r in (1, 2, 3)]
    gathered += [other_core(array) for array in gathered]
    attended, raised, per_row = forward(x)
    att = exchange(attended, ("z", "y_hi", "x"))
    grads = backward(x, raised, per_row)
    own, *sent = weight_terms(place, gathered, att)
    parts = [own] + [along_y(part, s) for s, part in enumerate(sent, 1)]
    home = exchange(grads, PATCH)
    columns, array = COLUMNS, jax.ShapeDtypeStruct
    own, *sent = small(
        sums_kernel, place, parts, [array((4, QUARTER, columns), F32)] * 4, [pltpu.VMEM((4, 4, QUARTER, columns), F32)]
    )
    parts = [own] + [along(part, "z", s) for s, part in enumerate(sent, 1)]
    mine, theirs = small(pick_kernel, place, parts, [array((4, 4, 11, columns), F32)] * 2)
    theirs = other_core(theirs)
    features = grad_out.shape[-1]
    own, *sent = small(
        join_kernel,
        place,
        (mine, theirs),
        [array((11, features), F32)] + [array((11, features), BF16)] * 3,
        [pltpu.VMEM((2, 4, 4, 11, columns), F32), pltpu.VMEM((4, 11, features), F32)],
    )
    parts = [own] + [along(part, "x", s) for s, part in enumerate(sent, 1)]
    *outs, grad_weight = unpack(home, parts, query_rows.shape)
    return (*outs, grad_weight)


def solution(mesh):
    chips = Mesh(mesh.devices.reshape(2, 4, 2, 4, 2), FRAME + PATCH)
    rows = P(FRAME, PATCH, None)
    return jax.shard_map(
        shards,
        mesh=chips,
        in_specs=(rows, rows, rows, rows, P()),
        out_specs=(rows, rows, rows, P(FRAME + PATCH, None)),
        check_vma=False,
    )
```
